512 devices in a mesh: wave: 64 (over z, x), lev: 8 (over y, core).
Axes of the slice: x: 4, y: 4, z: 16, core: 2. Of those that a mesh axis runs over, the one named last changes fastest.
Arguments:
- spectral: bfloat16 [64, 640, 2, 1024], P('wave', None, None, 'lev'), may hold values from -6 to 6
- legendre: bfloat16 [64, 1280, 640], P('wave'), may hold values from -0.25 to 0.25
- pattern: int32 [64, 10, 5], replicated, may hold values from 0 to 1, as said below
- assignment: int32 [64], replicated, may hold values from 0 to 63, each once
- quad_weight: float32 [1280], replicated, may hold values from 0.25 to 2
- coupling: bfloat16 [128, 128], replicated, may hold values from -1 to 2
Outputs:
- tendency: bfloat16 [64, 640, 2, 1024], P('wave', None, None, 'lev')
The draws below stay inside these ranges and needn't reach their ends.
Inputs may be any that keep to these rules, and one draw needn't show every extreme that they name: For each wavenumber m and degree block k, the latitude blocks with pattern 1 form a band symmetric about the equator that holds the two middle blocks; wavenumber 0 keeps all blocks.
All inputs are finite; a program needn't handle non-finite values.
Results may differ from the reference program's by a relative error of at most 0.0095.
Values may be sent and summed in bfloat16 or wider, within the bound.
No kernel may reach another device: no remote copies, remote signals or barrier semaphores. Data moves between devices by JAX's collectives and lax.ppermute only.
A program may use at most 64 MiB of HBM per device.

```python
import math
import jax
import jax.numpy as jnp
from jax import lax

LEV_DEV = 16
F = 8
NLAT = 1280
NN = 640
TILE = 128
M = 64
NLON = 192
LEV = 128
N_LEV = 8


def draw_pattern(key, part):
    lat_tiles = NLAT // TILE
    deg_tiles = NN // TILE
    waves = jnp.arange(M, dtype=jnp.int32)
    highest = waves * (lat_tiles // 2 - 1) // M + 1
    depth = jax.random.randint(key, (M, 1, deg_tiles), 0, highest[:, None, None])
    tiles = jnp.arange(lat_tiles, dtype=jnp.int32)
    distance = jnp.minimum(tiles, lat_tiles - 1 - tiles)
    return (distance[None, :, None] >= depth).astype(jnp.int32)


def draw_coupling(key, part):
    key_diagonal = jax.random.fold_in(key, 11)
    key_spread = jax.random.fold_in(key, 23)
    spread_part = jnp.clip(jax.random.normal(key_spread, (LEV, LEV), jnp.float32), -3.0, 3.0) * (0.6 / math.sqrt(LEV))
    diagonal_part = jax.random.uniform(key_diagonal, (LEV,), jnp.float32, 1.0, 1.5)
    return (spread_part + jnp.diag(diagonal_part)).astype(jnp.bfloat16)


def block_levels(own_key, extent, split, least, high):
    def one(position, parts):
        draws = jax.random.uniform(jax.random.fold_in(jax.random.fold_in(own_key, 6), position), (parts,), jnp.float32, least / len(split), high / len(split))
        return jnp.repeat(jnp.exp(draws), extent[position] // parts).reshape((-1,) + (1,) * (len(extent) - position - 1))

    loudness = one(*split[0])
    for cut in split[1:]:
        loudness = loudness * one(*cut)
    return loudness


def gaussian(own_key, shape, width, limit, shards=(), held_as=jnp.bfloat16):
    gain = block_levels(own_key, shape, shards, -0.22, 0.18) if shards else 1.0
    result = jax.random.normal(own_key, shape, jnp.float32) * width * gain
    return jnp.minimum(jnp.maximum(result, -limit), limit).astype(held_as)


def setup_inputs(seed: int = 0) -> dict:
    key_of = jax.random.split(jax.random.key(seed), 7)
    spectral = gaussian(key_of[0], (M, NN, 2, LEV * F), 1.0, 6.0, ((0, 64), (3, 8)))
    legendre = gaussian(key_of[1], (M, NLAT, NN), NN ** -0.5, 0.25, ((0, 64),))
    pattern = draw_pattern(jax.random.fold_in(key_of[6], 71), 0)
    assignment = jax.random.permutation(key_of[3], M).astype(jnp.int32)
    quad_weight = jnp.clip(jnp.exp(jax.random.uniform(key_of[4], (NLAT,), jnp.float32, math.log(0.25), math.log(2.0))), 0.25, 2.0)
    coupling = draw_coupling(jax.random.fold_in(key_of[6], 71), 0)
    return dict(spectral=spectral, legendre=legendre, pattern=pattern, assignment=assignment, quad_weight=quad_weight, coupling=coupling)


def expand_tiles(selected):
    return jnp.repeat(jnp.repeat(selected, TILE, axis=1), TILE, axis=2)

def dft_tables(wavenums, lon_count):
    wave_total = wavenums.shape[0]
    longitudes = jnp.arange(lon_count, dtype=jnp.int32)
    phases = longitudes[:, None] * wavenums[None, :].astype(jnp.int32) % lon_count
    angles = phases.astype(jnp.float32) * (2.0 * math.pi / lon_count)
    cosines = jnp.cos(angles)
    sines = jnp.sin(angles)
    synthesis = jnp.stack([cosines, -sines], axis=2).reshape(lon_count, 2 * wave_total) / math.sqrt(wave_total)
    analysis = jnp.stack([cosines.T, -sines.T], axis=1).reshape(2 * wave_total, lon_count) / math.sqrt(lon_count)
    return (synthesis.astype(jnp.bfloat16), analysis.astype(jnp.bfloat16))

def nonlinear(latitude_coeffs, synthesis, analysis, wave_total, channels):
    coeffs = latitude_coeffs.reshape(2 * wave_total, channels)
    field = jnp.dot(synthesis, coeffs, preferred_element_type=jnp.float32)
    shaped = field.reshape(field.shape[0], channels // F, F)
    product = (shaped * jnp.roll(shaped, -1, axis=2)).astype(jnp.bfloat16).reshape(field.shape[0], channels)
    returned = jnp.dot(analysis, product, preferred_element_type=jnp.float32)
    return returned.astype(jnp.bfloat16).reshape(wave_total, 2, channels)

def reference(spectral, legendre, pattern, assignment, quad_weight, coupling):
    wave_total = assignment.shape[0]
    channels = spectral.shape[3]
    lat_count = legendre.shape[1]
    degrees = legendre.shape[2]
    chosen = pattern[assignment].astype(jnp.bfloat16)
    pruned = legendre * expand_tiles(chosen)
    flattened = spectral.reshape(wave_total, degrees, 2 * channels)

    def forward(operands):
        matrix, coeffs = operands
        return jnp.dot(matrix, coeffs, preferred_element_type=jnp.float32).astype(jnp.bfloat16)
    at_lats = lax.map(forward, (pruned, flattened)).reshape(wave_total, lat_count, 2, channels)
    synthesis, analysis = dft_tables(assignment, NLON)

    def per_latitude(lat_index):
        column = lax.dynamic_index_in_dim(at_lats, lat_index, 1, keepdims=False)
        return nonlinear(column, synthesis, analysis, wave_total, channels)
    returned = lax.map(per_latitude, jnp.arange(lat_count, dtype=jnp.int32))
    weighted = (quad_weight[:, None, None, None] * returned.astype(jnp.float32)).astype(jnp.bfloat16)
    weighted = weighted.reshape(lat_count, wave_total, 2 * channels)

    def backward(operands):
        matrix, values = operands
        summed = lax.dot_general(matrix, values, (((0,), (0,)), ((), ())), preferred_element_type=jnp.float32)
        return summed.astype(jnp.bfloat16)
    spectral_new = lax.map(backward, (pruned, jnp.moveaxis(weighted, 1, 0)))
    levels = spectral_new.reshape(wave_total, degrees, 2, LEV, F)
    total = jnp.zeros((wave_total, degrees, 2, LEV, F), jnp.float32)
    for block_index in range(N_LEV):
        first_level = block_index * LEV_DEV
        columns = coupling[:, first_level:first_level + LEV_DEV].astype(jnp.float32)
        segment = levels[:, :, :, first_level:first_level + LEV_DEV, :].astype(jnp.float32)
        partial_sum = jnp.einsum('ab,sncbf->sncaf', columns, segment)
        total = total + lax.optimization_barrier(partial_sum.astype(jnp.bfloat16)).astype(jnp.float32)
    return total.reshape(wave_total, degrees, 2, channels).astype(jnp.bfloat16)
```

```python
import functools
import math

import jax
import jax.numpy as jnp
from jax import lax
from jax.experimental import pallas as pl
from jax.experimental.pallas import tpu as pltpu
from jax.sharding import Mesh
from jax.sharding import PartitionSpec as P

F = 8
TILE = 128
PEERS = ("y", "x", "z")
SIZES = {"z": 16, "x": 4, "y": 4, "core": 2}


def wave_tables(column_waves, lats, lon_count, wave_total):
    rows = wave_total * lats * 2
    longitudes = jnp.arange(lon_count, dtype=jnp.int32)
    phases = longitudes[:, None] * column_waves[None, :] % lon_count
    angles = phases.astype(jnp.float32) * (2.0 * math.pi / lon_count)
    imaginary = (jnp.arange(rows, dtype=jnp.int32) % 2 == 1)[None, :]
    basis = jnp.where(imaginary, -jnp.sin(angles), jnp.cos(angles))
    synthesis = (basis / math.sqrt(wave_total)).astype(jnp.bfloat16)
    phases_t = column_waves[:, None] * longitudes[None, :] % lon_count
    angles_t = phases_t.astype(jnp.float32) * (2.0 * math.pi / lon_count)
    basis_t = jnp.where(imaginary.T, -jnp.sin(angles_t), jnp.cos(angles_t))
    analysis = (basis_t / math.sqrt(lon_count)).astype(jnp.bfloat16)
    return synthesis, analysis


def grid_kernel(lats, received, synthesis, analysis, returned):
    blocks, rows, lanes = received.shape
    lon_count = synthesis.shape[0]
    column_lat = lax.broadcasted_iota(jnp.int32, (lon_count, rows), 1) // 2 % lats
    row_lat = lax.broadcasted_iota(jnp.int32, (rows, lon_count), 0) // 2 % lats
    step = 2
    for first in range(0, blocks, step):
        coeffs = jnp.concatenate([received[first + i] for i in range(step)], axis=1)
        width = step * lanes
        field_index = lax.broadcasted_iota(jnp.int32, (lon_count, width), 1) % F
        total = None
        for lat in range(lats):
            table = jnp.where(column_lat == lat, synthesis[...], jnp.zeros((), jnp.bfloat16))
            field = jnp.dot(table, coeffs, preferred_element_type=jnp.float32)
            following = pltpu.roll(field, width - 1, 1)
            wrapped = pltpu.roll(field, F - 1, 1)
            partner = jnp.where(field_index == F - 1, wrapped, following)
            product = (field * partner).astype(jnp.bfloat16)
            back = jnp.where(row_lat == lat, analysis[...], jnp.zeros((), jnp.bfloat16))
            term = jnp.dot(back, product, preferred_element_type=jnp.float32)
            total = term if total is None else total + term
        returned[:, first * lanes : (first + step) * lanes] = total.astype(jnp.bfloat16)


def couple_kernel(own, other, own_matrix, other_matrix, weight, sent):
    total = jnp.dot(own[...], own_matrix[...], preferred_element_type=jnp.float32)
    total += jnp.dot(other[...], other_matrix[...], preferred_element_type=jnp.float32)
    total *= weight[...]
    blocks, rows, lanes = sent.shape
    for i in range(blocks):
        sent[i] = total[:, i * lanes : (i + 1) * lanes].astype(jnp.bfloat16)


def call(kernel, out_shape, flops, limit, *operands):
    moved = sum(x.size * x.dtype.itemsize for x in operands) + out_shape.size * 2
    return pl.pallas_call(
        kernel,
        out_shape=out_shape,
        in_specs=[pl.BlockSpec(memory_space=pltpu.VMEM)] * len(operands),
        out_specs=pl.BlockSpec(memory_space=pltpu.VMEM),
        compiler_params=pltpu.CompilerParams(vmem_limit_bytes=limit << 20),
        cost_estimate=pl.CostEstimate(flops=flops, bytes_accessed=moved, transcendentals=0),
    )(*operands)


def local(spectral, legendre, pattern, assignment, quad_weight, coupling):
    degrees = spectral.shape[1]
    channels = spectral.shape[3]
    lat_count = legendre.shape[1]
    wave_total = assignment.shape[0]
    y_count = SIZES["y"]
    peers = y_count * wave_total
    lats = lat_count // peers
    rows = wave_total * lats * 2
    own_levels = channels // F
    slot = lax.axis_index("z") * SIZES["x"] + lax.axis_index("x")
    core = lax.axis_index("core")

    own_wave = lax.dynamic_index_in_dim(assignment, slot, 0, keepdims=False)
    own_mask = lax.dynamic_index_in_dim(pattern, own_wave, 0, keepdims=False).astype(jnp.bfloat16)
    lat_tiles, deg_tiles = own_mask.shape
    wide_mask = jnp.broadcast_to(
        own_mask[:, None, :, None], (lat_tiles, TILE, deg_tiles, TILE)
    ).reshape(lat_count, degrees)
    pruned = legendre[0] * wide_mask

    at_lats = jnp.einsum("ln,nch->lch", pruned, spectral[0], preferred_element_type=jnp.float32)
    at_lats = at_lats.astype(jnp.bfloat16).reshape(peers, lats, 2, channels)
    received = lax.all_to_all(at_lats, PEERS, split_axis=0, concat_axis=0, tiled=True)
    received = received.reshape(y_count, rows, channels)

    arrival = assignment.reshape(SIZES["z"], SIZES["x"]).T.reshape(wave_total)
    column_waves = jnp.broadcast_to(arrival[:, None], (wave_total, lats * 2)).reshape(rows)
    lon_count = 3 * wave_total
    synthesis, analysis = wave_tables(column_waves, lats, lon_count, wave_total)
    cores = SIZES["core"]
    split = coupling.reshape(y_count, cores, own_levels, y_count, cores, own_levels)
    mine = lax.dynamic_index_in_dim(split, core, 1, keepdims=False)
    wide = y_count * channels
    spread = (
        jnp.arange(wide, dtype=jnp.int32)[:, None] // F
        == jnp.arange(wide // F, dtype=jnp.int32)[None, :]
    ).astype(jnp.bfloat16)
    same_field = (
        jnp.arange(wide, dtype=jnp.int32)[:, None] % F
        == jnp.arange(wide, dtype=jnp.int32)[None, :] % F
    )

    def matrix(source):
        small = lax.dynamic_index_in_dim(mine, source, 3, keepdims=False)
        small = small.reshape(wide // F, wide // F)
        tall = jnp.einsum("pb,ab->pa", spread, small).astype(jnp.bfloat16)
        full = jnp.einsum("pa,qa->pq", tall, spread).astype(jnp.bfloat16)
        return jnp.where(same_field, full, jnp.zeros((), jnp.bfloat16))

    group = lax.axis_index(PEERS)
    weight = lax.dynamic_slice_in_dim(quad_weight, group * lats, lats)
    weight = jnp.broadcast_to(weight[None, :, None], (wave_total, lats, 2)).reshape(rows, 1)
    own_matrix, other_matrix = matrix(core), matrix(1 - core)
    received, synthesis, analysis, own_matrix, other_matrix, weight = lax.optimization_barrier(
        (received, synthesis, analysis, own_matrix, other_matrix, weight)
    )

    flops = 4 * lats * lon_count * rows * y_count * channels
    returned = call(
        functools.partial(grid_kernel, lats),
        jax.ShapeDtypeStruct((rows, y_count * channels), jnp.bfloat16),
        flops,
        16,
        received,
        synthesis,
        analysis,
    )
    swapped = lax.ppermute(returned, "core", [(0, 1), (1, 0)])

    sent = call(
        couple_kernel,
        jax.ShapeDtypeStruct((y_count, rows, channels), jnp.bfloat16),
        4 * rows * wide * wide,
        16,
        returned,
        swapped,
        own_matrix,
        other_matrix,
        weight,
    )
    sent = sent.reshape(peers, lats, 2, channels)
    weighted = lax.all_to_all(sent, PEERS, split_axis=0, concat_axis=0, tiled=True)
    weighted = weighted.reshape(lat_count, 2, channels)
    tendency = jnp.einsum("ln,lch->nch", pruned, weighted, preferred_element_type=jnp.float32)
    return tendency.astype(jnp.bfloat16)[None]


def solution(mesh):
    grid = Mesh(mesh.devices.reshape(tuple(SIZES.values())), tuple(SIZES))
    wave, lev = ("z", "x"), ("y", "core")
    placed = (P(wave, None, None, lev), P(wave, None, None), P(), P(), P(), P())
    return jax.shard_map(
        local,
        mesh=grid,
        in_specs=placed,
        out_specs=P(wave, None, None, lev),
        check_vma=False,
    )
```

```python
import functools
import math

import jax
import jax.numpy as jnp
from jax import lax
from jax.experimental import pallas as pl
from jax.experimental.pallas import tpu as pltpu
from jax.sharding import Mesh
from jax.sharding import PartitionSpec as P

F = 8
TILE = 128
LAT_CHUNKS = 5
PEERS = ("y", "x", "z")
SIZES = {"z": 16, "x": 4, "y": 4, "core": 2}


def wave_tables(column_waves, lats, lon_count, wave_total):
    rows = wave_total * lats * 2
    longitudes = jnp.arange(lon_count, dtype=jnp.int32)
    phases = longitudes[:, None] * column_waves[None, :] % lon_count
    angles = phases.astype(jnp.float32) * (2.0 * math.pi / lon_count)
    imaginary = (jnp.arange(rows, dtype=jnp.int32) % 2 == 1)[None, :]
    basis = jnp.where(imaginary, -jnp.sin(angles), jnp.cos(angles))
    synthesis = (basis / math.sqrt(wave_total)).astype(jnp.bfloat16)
    phases_t = column_waves[:, None] * longitudes[None, :] % lon_count
    angles_t = phases_t.astype(jnp.float32) * (2.0 * math.pi / lon_count)
    basis_t = jnp.where(imaginary.T, -jnp.sin(angles_t), jnp.cos(angles_t))
    analysis = (basis_t / math.sqrt(lon_count)).astype(jnp.bfloat16)
    return synthesis, analysis


def even_odd(size):
    row = lax.broadcasted_iota(jnp.int32, (size, 2 * size), 0)
    column = lax.broadcasted_iota(jnp.int32, (size, 2 * size), 1)
    return [(column == 2 * row + part).astype(jnp.bfloat16) for part in range(2)]


def merge(size):
    row = lax.broadcasted_iota(jnp.int32, (2 * size, 2 * size), 0)
    column = lax.broadcasted_iota(jnp.int32, (2 * size, 2 * size), 1)
    return (column == row % 2 * size + row // 2).astype(jnp.bfloat16)


def forward_kernel(
    spectral, legendre, pattern, assignment, at_lats, raw, matrix, coeffs, merged, in_sem, lat_sem, out_sem
):
    lat_tiles, deg_tiles, _ = pattern.shape
    raw_copy = pltpu.make_async_copy(spectral, raw, in_sem)
    raw_copy.start()
    chunk = TILE * lat_tiles // LAT_CHUNKS

    def lat_copy(i):
        span = pl.ds(i * chunk, chunk)
        return pltpu.make_async_copy(legendre.at[span], matrix.at[span], lat_sem.at[i])

    for i in range(LAT_CHUNKS):
        lat_copy(i).start()
    slot = lax.axis_index("z") * SIZES["x"] + lax.axis_index("x")
    wave = assignment[slot]
    picked = lax.broadcasted_iota(jnp.int32, pattern.shape, 2) == wave
    mask = jnp.sum(jnp.where(picked, pattern[...], 0), axis=2, keepdims=True)
    halves = even_odd(TILE)
    lanes = raw.shape[1]
    raw_copy.wait()
    for k in range(deg_tiles):
        block = raw[2 * TILE * k : 2 * TILE * (k + 1), :]
        for part in range(2):
            coeffs[TILE * k : TILE * (k + 1), lanes * part : lanes * (part + 1)] = jnp.dot(
                halves[part], block, preferred_element_type=jnp.float32
            ).astype(jnp.bfloat16)
    order = merge(TILE)

    def out_copy(i):
        span = pl.ds(2 * i * chunk, 2 * chunk)
        return pltpu.make_async_copy(merged.at[span], at_lats.at[span], out_sem.at[i])

    for i in range(LAT_CHUNKS):
        lat_copy(i).wait()
        for t in range(i * lat_tiles // LAT_CHUNKS, (i + 1) * lat_tiles // LAT_CHUNKS):
            keep = jnp.concatenate(
                [
                    jnp.broadcast_to(mask[t, k : k + 1, :], (TILE, TILE)).astype(jnp.bfloat16)
                    for k in range(deg_tiles)
                ],
                axis=1,
            )
            pruned = matrix[TILE * t : TILE * (t + 1), :] * keep
            found = jnp.dot(pruned, coeffs[...], preferred_element_type=jnp.float32)
            found = found.astype(jnp.bfloat16)
            stacked = jnp.concatenate([found[:, :lanes], found[:, lanes:]], axis=0)
            merged[2 * TILE * t : 2 * TILE * (t + 1), :] = jnp.dot(
                order, stacked, preferred_element_type=jnp.float32
            ).astype(jnp.bfloat16)
        out_copy(i).start()
    for i in range(LAT_CHUNKS):
        out_copy(i).wait()


def forward(spectral, legendre, pattern, assignment):
    degrees, _, channels = spectral.shape
    lat_count = legendre.shape[0]
    anywhere = pl.BlockSpec(memory_space=pl.ANY)
    return pl.pallas_call(
        forward_kernel,
        out_shape=jax.ShapeDtypeStruct((2 * lat_count, channels), jnp.bfloat16),
        in_specs=[
            anywhere,
            anywhere,
            pl.BlockSpec(memory_space=pltpu.VMEM),
            pl.BlockSpec(memory_space=pltpu.SMEM),
        ],
        out_specs=anywhere,
        scratch_shapes=[
            pltpu.VMEM((2 * degrees, channels), jnp.bfloat16),
            pltpu.VMEM((lat_count, degrees), jnp.bfloat16),
            pltpu.VMEM((degrees, 2 * channels), jnp.bfloat16),
            pltpu.VMEM((2 * lat_count, channels), jnp.bfloat16),
            pltpu.SemaphoreType.DMA,
            pltpu.SemaphoreType.DMA((LAT_CHUNKS,)),
            pltpu.SemaphoreType.DMA((LAT_CHUNKS,)),
        ],
        compiler_params=pltpu.CompilerParams(vmem_limit_bytes=16 << 20),
    )(
        spectral.reshape(2 * degrees, channels),
        legendre,
        jnp.transpose(pattern, (1, 2, 0)),
        assignment,
    )


def grid_kernel(lats, received, synthesis, analysis, returned):
    blocks, rows, lanes = received.shape
    lon_count = synthesis.shape[0]
    column_lat = lax.broadcasted_iota(jnp.int32, (lon_count, rows), 1) // 2 % lats
    row_lat = lax.broadcasted_iota(jnp.int32, (rows, lon_count), 0) // 2 % lats
    step = 2
    for first in range(0, blocks, step):
        coeffs = jnp.concatenate([received[first + i] for i in range(step)], axis=1)
        width = step * lanes
        field_index = lax.broadcasted_iota(jnp.int32, (lon_count, width), 1) % F
        total = None
        for lat in range(lats):
            table = jnp.where(column_lat == lat, synthesis[...], jnp.zeros((), jnp.bfloat16))
            field = jnp.dot(table, coeffs, preferred_element_type=jnp.float32)
            following = pltpu.roll(field, width - 1, 1)
            wrapped = pltpu.roll(field, F - 1, 1)
            partner = jnp.where(field_index == F - 1, wrapped, following)
            product = (field * partner).astype(jnp.bfloat16)
            back = jnp.where(row_lat == lat, analysis[...], jnp.zeros((), jnp.bfloat16))
            term = jnp.dot(back, product, preferred_element_type=jnp.float32)
            total = term if total is None else total + term
        returned[:, first * lanes : (first + step) * lanes] = total.astype(jnp.bfloat16)


def couple_kernel(own, other, own_matrix, other_matrix, weight, sent):
    total = jnp.dot(own[...], own_matrix[...], preferred_element_type=jnp.float32)
    total += jnp.dot(other[...], other_matrix[...], preferred_element_type=jnp.float32)
    total *= weight[...]
    blocks, rows, lanes = sent.shape
    for i in range(blocks):
        sent[i] = total[:, i * lanes : (i + 1) * lanes].astype(jnp.bfloat16)


def call(kernel, out_shape, flops, limit, *operands):
    moved = sum(x.size * x.dtype.itemsize for x in operands) + out_shape.size * 2
    return pl.pallas_call(
        kernel,
        out_shape=out_shape,
        in_specs=[pl.BlockSpec(memory_space=pltpu.VMEM)] * len(operands),
        out_specs=pl.BlockSpec(memory_space=pltpu.VMEM),
        compiler_params=pltpu.CompilerParams(vmem_limit_bytes=limit << 20),
        cost_estimate=pl.CostEstimate(flops=flops, bytes_accessed=moved, transcendentals=0),
    )(*operands)


def local(spectral, legendre, pattern, assignment, quad_weight, coupling):
    degrees = spectral.shape[1]
    channels = spectral.shape[3]
    lat_count = legendre.shape[1]
    wave_total = assignment.shape[0]
    y_count = SIZES["y"]
    peers = y_count * wave_total
    lats = lat_count // peers
    rows = wave_total * lats * 2
    own_levels = channels // F
    slot = lax.axis_index("z") * SIZES["x"] + lax.axis_index("x")
    core = lax.axis_index("core")

    own_wave = lax.dynamic_index_in_dim(assignment, slot, 0, keepdims=False)
    own_mask = lax.dynamic_index_in_dim(pattern, own_wave, 0, keepdims=False).astype(jnp.bfloat16)
    lat_tiles, deg_tiles = own_mask.shape
    wide_mask = jnp.broadcast_to(
        own_mask[:, None, :, None], (lat_tiles, TILE, deg_tiles, TILE)
    ).reshape(lat_count, degrees)
    pruned = legendre[0] * wide_mask

    at_lats = forward(spectral[0], legendre[0], pattern, assignment)
    at_lats = at_lats.reshape(peers, lats, 2, channels)
    received = lax.all_to_all(at_lats, PEERS, split_axis=0, concat_axis=0, tiled=True)
    received = received.reshape(y_count, rows, channels)

    arrival = assignment.reshape(SIZES["z"], SIZES["x"]).T.reshape(wave_total)
    column_waves = jnp.broadcast_to(arrival[:, None], (wave_total, lats * 2)).reshape(rows)
    lon_count = 3 * wave_total
    synthesis, analysis = wave_tables(column_waves, lats, lon_count, wave_total)
    cores = SIZES["core"]
    split = coupling.reshape(y_count, cores, own_levels, y_count, cores, own_levels)
    mine = lax.dynamic_index_in_dim(split, core, 1, keepdims=False)
    wide = y_count * channels
    spread = (
        jnp.arange(wide, dtype=jnp.int32)[:, None] // F
        == jnp.arange(wide // F, dtype=jnp.int32)[None, :]
    ).astype(jnp.bfloat16)
    same_field = (
        jnp.arange(wide, dtype=jnp.int32)[:, None] % F
        == jnp.arange(wide, dtype=jnp.int32)[None, :] % F
    )

    def matrix(source):
        small = lax.dynamic_index_in_dim(mine, source, 3, keepdims=False)
        small = small.reshape(wide // F, wide // F)
        tall = jnp.einsum("pb,ab->pa", spread, small).astype(jnp.bfloat16)
        full = jnp.einsum("pa,qa->pq", tall, spread).astype(jnp.bfloat16)
        return jnp.where(same_field, full, jnp.zeros((), jnp.bfloat16))

    group = lax.axis_index(PEERS)
    weight = lax.dynamic_slice_in_dim(quad_weight, group * lats, lats)
    weight = jnp.broadcast_to(weight[None, :, None], (wave_total, lats, 2)).reshape(rows, 1)
    own_matrix, other_matrix = matrix(core), matrix(1 - core)
    received, synthesis, analysis, own_matrix, other_matrix, weight, pruned = (
        lax.optimization_barrier(
            (received, synthesis, analysis, own_matrix, other_matrix, weight, pruned)
        )
    )

    flops = 4 * lats * lon_count * rows * y_count * channels
    returned = call(
        functools.partial(grid_kernel, lats),
        jax.ShapeDtypeStruct((rows, y_count * channels), jnp.bfloat16),
        flops,
        16,
        received,
        synthesis,
        analysis,
    )
    swapped = lax.ppermute(returned, "core", [(0, 1), (1, 0)])

    sent = call(
        couple_kernel,
        jax.ShapeDtypeStruct((y_count, rows, channels), jnp.bfloat16),
        4 * rows * wide * wide,
        16,
        returned,
        swapped,
        own_matrix,
        other_matrix,
        weight,
    )
    sent = sent.reshape(peers, lats, 2, channels)
    weighted = lax.all_to_all(sent, PEERS, split_axis=0, concat_axis=0, tiled=True)
    weighted = weighted.reshape(lat_count, 2, channels)
    tendency = jnp.einsum("ln,lch->nch", pruned, weighted, preferred_element_type=jnp.float32)
    return tendency.astype(jnp.bfloat16)[None]


def solution(mesh):
    grid = Mesh(mesh.devices.reshape(tuple(SIZES.values())), tuple(SIZES))
    wave, lev = ("z", "x"), ("y", "core")
    placed = (P(wave, None, None, lev), P(wave, None, None), P(), P(), P(), P())
    return jax.shard_map(
        local,
        mesh=grid,
        in_specs=placed,
        out_specs=P(wave, None, None, lev),
        check_vma=False,
    )
```

```python
import functools
import math

import jax
import jax.numpy as jnp
from jax import lax
from jax.experimental import pallas as pl
from jax.experimental.pallas import tpu as pltpu
from jax.sharding import Mesh
from jax.sharding import PartitionSpec as P

F = 8
TILE = 128
LAT_CHUNKS = 2
PEERS = ("y", "x", "z")
SIZES = {"z": 16, "x": 4, "y": 4, "core": 2}


def wave_tables(waves, lon_count):
    wave_total = waves.shape[0]
    longitudes = jnp.arange(lon_count, dtype=jnp.int32)
    phases = longitudes[:, None] * waves[None, :] % lon_count
    angles = phases.astype(jnp.float32) * (2.0 * math.pi / lon_count)
    basis = jnp.concatenate([jnp.cos(angles), -jnp.sin(angles)], axis=1)
    synthesis = (basis / math.sqrt(wave_total)).astype(jnp.bfloat16)
    analysis = (basis.T / math.sqrt(lon_count)).astype(jnp.bfloat16)
    return synthesis, analysis


def forward_kernel(
    spectral, legendre, pattern, assignment, at_lats,
    raw, matrix, blocks, waves, paired, coeffs, wide, merged, in_sem, lat_sem, out_sem,
):
    lat_tiles, deg_tiles, _ = pattern.shape
    lat_count, degrees = legendre.shape
    lanes = raw.shape[1]
    chunk = lat_count // LAT_CHUNKS
    copies = [
        pltpu.make_async_copy(source, target, in_sem.at[i])
        for i, (source, target) in enumerate(
            ((spectral, raw), (assignment, waves), (pattern, blocks))
        )
    ]
    for copy in copies:
        copy.start()

    def lat_copy(i):
        span = pl.ds(i * chunk, chunk)
        return pltpu.make_async_copy(legendre.at[span], matrix.at[span], lat_sem.at[i])

    def out_copy(i):
        span = pl.ds(2 * i * chunk, 2 * chunk)
        return pltpu.make_async_copy(merged.at[span], at_lats.at[span], out_sem.at[i])

    for i in range(LAT_CHUNKS):
        lat_copy(i).start()
    copies[0].wait()
    paired[...] = raw[...].astype(jnp.float32)
    for part in range(2):
        coeffs[:, part * lanes : (part + 1) * lanes] = paired[
            pl.ds(part, degrees, stride=2), :
        ].astype(jnp.bfloat16)
    copies[1].wait()
    copies[2].wait()
    slot = lax.axis_index("z") * SIZES["x"] + lax.axis_index("x")
    wave = waves[slot]
    picked = lax.broadcasted_iota(jnp.int32, blocks.shape, 2) == wave
    mask = jnp.sum(jnp.where(picked, blocks[...], 0), axis=2, keepdims=True)
    for i in range(LAT_CHUNKS):
        lat_copy(i).wait()
        for t in range(i * lat_tiles // LAT_CHUNKS, (i + 1) * lat_tiles // LAT_CHUNKS):
            keep = jnp.concatenate(
                [
                    jnp.broadcast_to(mask[t, k : k + 1, :], (TILE, TILE)).astype(jnp.bfloat16)
                    for k in range(deg_tiles)
                ],
                axis=1,
            )
            tile = slice(TILE * t, TILE * (t + 1))
            matrix[tile, :] = matrix[tile, :] * keep
        found = jnp.dot(
            matrix[chunk * i : chunk * (i + 1), :],
            coeffs[...],
            preferred_element_type=jnp.float32,
        )
        for part in range(2):
            wide[pl.ds(part, chunk, stride=2), :] = found[:, part * lanes : (part + 1) * lanes]
        merged[2 * chunk * i : 2 * chunk * (i + 1), :] = wide[...].astype(jnp.bfloat16)
        out_copy(i).start()
    for i in range(LAT_CHUNKS):
        out_copy(i).wait()


def forward(spectral, legendre, pattern, assignment):
    degrees, _, channels = spectral.shape
    lat_count = legendre.shape[0]
    pattern = jnp.transpose(pattern, (1, 2, 0))
    chunk = lat_count // LAT_CHUNKS
    return pl.pallas_call(
        forward_kernel,
        out_shape=jax.ShapeDtypeStruct((2 * lat_count, channels), jnp.bfloat16),
        in_specs=[pl.BlockSpec(memory_space=pltpu.HBM)] * 4,
        out_specs=pl.BlockSpec(memory_space=pltpu.HBM),
        scratch_shapes=[
            pltpu.VMEM((2 * degrees, channels), jnp.bfloat16),
            pltpu.VMEM((lat_count, degrees), jnp.bfloat16),
            pltpu.VMEM(pattern.shape, jnp.int32),
            pltpu.SMEM(assignment.shape, jnp.int32),
            pltpu.VMEM((2 * degrees, channels), jnp.float32),
            pltpu.VMEM((degrees, 2 * channels), jnp.bfloat16),
            pltpu.VMEM((2 * chunk, channels), jnp.float32),
            pltpu.VMEM((2 * lat_count, channels), jnp.bfloat16),
            pltpu.SemaphoreType.DMA((3,)),
            pltpu.SemaphoreType.DMA((LAT_CHUNKS,)),
            pltpu.SemaphoreType.DMA((LAT_CHUNKS,)),
        ],
        compiler_params=pltpu.CompilerParams(vmem_limit_bytes=16 << 20),
    )(spectral.reshape(2 * degrees, channels), legendre, pattern, assignment)


def grid_kernel(lats, received, synthesis, analysis, returned, wide):
    blocks, rows, lanes = received.shape
    width = blocks * lanes
    slots = rows // (2 * lats)
    wide[...] = received[...].astype(jnp.float32)
    last_field = lax.broadcasted_iota(jnp.int32, (synthesis.shape[0], width), 1) % F == F - 1

    def span(lat, part):
        return pl.ds(2 * lat + part, slots, stride=2 * lats)

    for lat in range(lats):
        coeffs = jnp.concatenate(
            [
                jnp.concatenate([wide[i, span(lat, part), :] for i in range(blocks)], axis=1)
                for part in range(2)
            ],
            axis=0,
        ).astype(jnp.bfloat16)
        field = jnp.dot(synthesis[...], coeffs, preferred_element_type=jnp.float32)
        following = pltpu.roll(field, width - 1, 1)
        wrapped = pltpu.roll(field, F - 1, 1)
        product = (field * jnp.where(last_field, wrapped, following)).astype(jnp.bfloat16)
        back = jnp.dot(analysis[...], product, preferred_element_type=jnp.float32)
        for part in range(2):
            for i in range(blocks):
                wide[i, span(lat, part), :] = back[
                    part * slots : (part + 1) * slots, i * lanes : (i + 1) * lanes
                ]
    for i in range(blocks):
        returned[:, i * lanes : (i + 1) * lanes] = wide[i].astype(jnp.bfloat16)


def couple_kernel(own, other, own_matrix, other_matrix, weight, sent):
    total = jnp.dot(own[...], own_matrix[...], preferred_element_type=jnp.float32)
    total += jnp.dot(other[...], other_matrix[...], preferred_element_type=jnp.float32)
    total *= weight[...]
    blocks, rows, lanes = sent.shape
    for i in range(blocks):
        sent[i] = total[:, i * lanes : (i + 1) * lanes].astype(jnp.bfloat16)


def call(kernel, out_shape, flops, limit, *operands, scratch=()):
    moved = sum(x.size * x.dtype.itemsize for x in operands) + out_shape.size * 2
    return pl.pallas_call(
        kernel,
        out_shape=out_shape,
        in_specs=[pl.BlockSpec(memory_space=pltpu.VMEM)] * len(operands),
        out_specs=pl.BlockSpec(memory_space=pltpu.VMEM),
        scratch_shapes=scratch,
        compiler_params=pltpu.CompilerParams(vmem_limit_bytes=limit << 20),
        cost_estimate=pl.CostEstimate(flops=flops, bytes_accessed=moved, transcendentals=0),
    )(*operands)


def local(spectral, legendre, pattern, assignment, quad_weight, coupling):
    degrees = spectral.shape[1]
    channels = spectral.shape[3]
    lat_count = legendre.shape[1]
    wave_total = assignment.shape[0]
    y_count = SIZES["y"]
    peers = y_count * wave_total
    lats = lat_count // peers
    rows = wave_total * lats * 2
    own_levels = channels // F
    slot = lax.axis_index("z") * SIZES["x"] + lax.axis_index("x")
    core = lax.axis_index("core")

    own_wave = lax.dynamic_index_in_dim(assignment, slot, 0, keepdims=False)
    own_mask = lax.dynamic_index_in_dim(pattern, own_wave, 0, keepdims=False).astype(jnp.bfloat16)
    lat_tiles, deg_tiles = own_mask.shape
    wide_mask = jnp.broadcast_to(
        own_mask[:, None, :, None], (lat_tiles, TILE, deg_tiles, TILE)
    ).reshape(lat_count, degrees)
    pruned = legendre[0] * wide_mask

    at_lats = forward(spectral[0], legendre[0], pattern, assignment)
    at_lats = at_lats.reshape(peers, lats, 2, channels)
    received = lax.all_to_all(at_lats, PEERS, split_axis=0, concat_axis=0, tiled=True)
    received = received.reshape(y_count, rows, channels)

    arrival = assignment.reshape(SIZES["z"], SIZES["x"]).T.reshape(wave_total)
    lon_count = 3 * wave_total
    synthesis, analysis = wave_tables(arrival, lon_count)
    cores = SIZES["core"]
    split = coupling.reshape(y_count, cores, own_levels, y_count, cores, own_levels)
    mine = lax.dynamic_index_in_dim(split, core, 1, keepdims=False)
    wide = y_count * channels
    spread = (
        jnp.arange(wide, dtype=jnp.int32)[:, None] // F
        == jnp.arange(wide // F, dtype=jnp.int32)[None, :]
    ).astype(jnp.bfloat16)
    same_field = (
        jnp.arange(wide, dtype=jnp.int32)[:, None] % F
        == jnp.arange(wide, dtype=jnp.int32)[None, :] % F
    )

    def matrix(source):
        small = lax.dynamic_index_in_dim(mine, source, 3, keepdims=False)
        small = small.reshape(wide // F, wide // F)
        tall = jnp.einsum("pb,ab->pa", spread, small).astype(jnp.bfloat16)
        full = jnp.einsum("pa,qa->pq", tall, spread).astype(jnp.bfloat16)
        return jnp.where(same_field, full, jnp.zeros((), jnp.bfloat16))

    group = lax.axis_index(PEERS)
    weight = lax.dynamic_slice_in_dim(quad_weight, group * lats, lats)
    weight = jnp.broadcast_to(weight[None, :, None], (wave_total, lats, 2)).reshape(rows, 1)
    own_matrix, other_matrix = matrix(core), matrix(1 - core)
    received, synthesis, analysis, own_matrix, other_matrix, weight, pruned = (
        lax.optimization_barrier(
            (received, synthesis, analysis, own_matrix, other_matrix, weight, pruned)
        )
    )

    wide = y_count * channels
    flops = 4 * lon_count * rows * wide
    returned = call(
        functools.partial(grid_kernel, lats),
        jax.ShapeDtypeStruct((rows, wide), jnp.bfloat16),
        flops,
        16,
        received,
        synthesis,
        analysis,
        scratch=[pltpu.VMEM((y_count, rows, channels), jnp.float32)],
    )
    swapped = lax.ppermute(returned, "core", [(0, 1), (1, 0)])

    sent = call(
        couple_kernel,
        jax.ShapeDtypeStruct((y_count, rows, channels), jnp.bfloat16),
        4 * rows * wide * wide,
        16,
        returned,
        swapped,
        own_matrix,
        other_matrix,
        weight,
    )
    sent = sent.reshape(peers, lats, 2, channels)
    weighted = lax.all_to_all(sent, PEERS, split_axis=0, concat_axis=0, tiled=True)
    weighted = weighted.reshape(lat_count, 2, channels)
    tendency = jnp.einsum("ln,lch->nch", pruned, weighted, preferred_element_type=jnp.float32)
    return tendency.astype(jnp.bfloat16)[None]


def solution(mesh):
    grid = Mesh(mesh.devices.reshape(tuple(SIZES.values())), tuple(SIZES))
    wave, lev = ("z", "x"), ("y", "core")
    placed = (P(wave, None, None, lev), P(wave, None, None), P(), P(), P(), P())
    return jax.shard_map(
        local,
        mesh=grid,
        in_specs=placed,
        out_specs=P(wave, None, None, lev),
        check_vma=False,
    )
```

```python
import functools
import math

import jax
import jax.numpy as jnp
from jax import lax
from jax.experimental import pallas as pl
from jax.experimental.pallas import tpu as pltpu
from jax.sharding import Mesh
from jax.sharding import PartitionSpec as P

F = 8
TILE = 128
LAT_CHUNKS = 2
PEERS = ("y", "x", "z")
SIZES = {"z": 16, "x": 4, "y": 4, "core": 2}


def wave_tables(waves, lon_count):
    wave_total = waves.shape[0]
    longitudes = jnp.arange(lon_count, dtype=jnp.int32)
    phases = longitudes[:, None] * waves[None, :] % lon_count
    angles = phases.astype(jnp.float32) * (2.0 * math.pi / lon_count)
    basis = jnp.concatenate([jnp.cos(angles), -jnp.sin(angles)], axis=1)
    synthesis = (basis / math.sqrt(wave_total)).astype(jnp.bfloat16)
    analysis = (basis.T / math.sqrt(lon_count)).astype(jnp.bfloat16)
    return synthesis, analysis


def forward_kernel(
    spectral, legendre, pattern, assignment, at_lats,
    raw, matrix, blocks, waves, paired, coeffs, wide, merged, in_sem, lat_sem, out_sem,
):
    lat_tiles, deg_tiles, _ = pattern.shape
    lat_count, degrees = legendre.shape
    lanes = raw.shape[1]
    chunk = lat_count // LAT_CHUNKS
    copies = [
        pltpu.make_async_copy(source, target, in_sem.at[i])
        for i, (source, target) in enumerate(
            ((spectral, raw), (assignment, waves), (pattern, blocks))
        )
    ]
    for copy in copies:
        copy.start()

    def lat_copy(i):
        span = pl.ds(i * chunk, chunk)
        return pltpu.make_async_copy(legendre.at[span], matrix.at[span], lat_sem.at[i])

    def out_copy(i):
        span = pl.ds(2 * i * chunk, 2 * chunk)
        return pltpu.make_async_copy(merged.at[span], at_lats.at[span], out_sem.at[i])

    for i in range(LAT_CHUNKS):
        lat_copy(i).start()
    copies[0].wait()
    paired[...] = raw[...].astype(jnp.float32)
    for part in range(2):
        coeffs[:, part * lanes : (part + 1) * lanes] = paired[
            pl.ds(part, degrees, stride=2), :
        ].astype(jnp.bfloat16)
    copies[1].wait()
    copies[2].wait()
    slot = lax.axis_index("z") * SIZES["x"] + lax.axis_index("x")
    wave = waves[slot]
    picked = lax.broadcasted_iota(jnp.int32, blocks.shape, 2) == wave
    mask = jnp.sum(jnp.where(picked, blocks[...], 0), axis=2, keepdims=True)
    for i in range(LAT_CHUNKS):
        lat_copy(i).wait()
        for t in range(i * lat_tiles // LAT_CHUNKS, (i + 1) * lat_tiles // LAT_CHUNKS):
            keep = jnp.concatenate(
                [
                    jnp.broadcast_to(mask[t, k : k + 1, :], (TILE, TILE)).astype(jnp.bfloat16)
                    for k in range(deg_tiles)
                ],
                axis=1,
            )
            tile = slice(TILE * t, TILE * (t + 1))
            matrix[tile, :] = matrix[tile, :] * keep
        found = jnp.dot(
            matrix[chunk * i : chunk * (i + 1), :],
            coeffs[...],
            preferred_element_type=jnp.float32,
        )
        for part in range(2):
            wide[pl.ds(part, chunk, stride=2), :] = found[:, part * lanes : (part + 1) * lanes]
        merged[2 * chunk * i : 2 * chunk * (i + 1), :] = wide[...].astype(jnp.bfloat16)
        out_copy(i).start()
    for i in range(LAT_CHUNKS):
        out_copy(i).wait()


def forward(spectral, legendre, pattern, assignment):
    degrees, _, channels = spectral.shape
    lat_count = legendre.shape[0]
    pattern = jnp.transpose(pattern, (1, 2, 0))
    chunk = lat_count // LAT_CHUNKS
    return pl.pallas_call(
        forward_kernel,
        out_shape=jax.ShapeDtypeStruct((2 * lat_count, channels), jnp.bfloat16),
        in_specs=[pl.BlockSpec(memory_space=pltpu.HBM)] * 4,
        out_specs=pl.BlockSpec(memory_space=pltpu.HBM),
        scratch_shapes=[
            pltpu.VMEM((2 * degrees, channels), jnp.bfloat16),
            pltpu.VMEM((lat_count, degrees), jnp.bfloat16),
            pltpu.VMEM(pattern.shape, jnp.int32),
            pltpu.SMEM(assignment.shape, jnp.int32),
            pltpu.VMEM((2 * degrees, channels), jnp.float32),
            pltpu.VMEM((degrees, 2 * channels), jnp.bfloat16),
            pltpu.VMEM((2 * chunk, channels), jnp.float32),
            pltpu.VMEM((2 * lat_count, channels), jnp.bfloat16),
            pltpu.SemaphoreType.DMA((3,)),
            pltpu.SemaphoreType.DMA((LAT_CHUNKS,)),
            pltpu.SemaphoreType.DMA((LAT_CHUNKS,)),
        ],
    )(spectral.reshape(2 * degrees, channels), legendre, pattern, assignment)


def grid_kernel(lats, received, synthesis, analysis, returned, wide, ahead):
    blocks, rows, lanes = received.shape
    width = blocks * lanes
    slots = rows // (2 * lats)
    wide[...] = received[...].astype(jnp.float32)
    pair = 2 * lanes
    source = lax.broadcasted_iota(jnp.int32, (pair, pair), 0)
    target = lax.broadcasted_iota(jnp.int32, (pair, pair), 1)
    advance = (source == target // F * F + (target + 1) % F).astype(jnp.bfloat16)
    for i in range(0, blocks, 2):
        both = jnp.concatenate([received[i], received[i + 1]], axis=1)
        moved = jnp.dot(both, advance, preferred_element_type=jnp.float32)
        ahead[i] = moved[:, :lanes]
        ahead[i + 1] = moved[:, lanes:]

    def span(lat, part):
        return pl.ds(2 * lat + part, slots, stride=2 * lats)

    def gather(rows_of, lat):
        parts = [
            jnp.concatenate([rows_of[i, span(lat, part), :] for i in range(blocks)], axis=1)
            for part in range(2)
        ]
        return jnp.concatenate(parts, axis=0).astype(jnp.bfloat16)

    for lat in range(lats):
        field, partner = (
            jnp.dot(synthesis[...], gather(rows_of, lat), preferred_element_type=jnp.float32)
            for rows_of in (wide, ahead)
        )
        product = (field * partner).astype(jnp.bfloat16)
        back = jnp.dot(analysis[...], product, preferred_element_type=jnp.float32)
        for part in range(2):
            for i in range(blocks):
                wide[i, span(lat, part), :] = back[
                    part * slots : (part + 1) * slots, i * lanes : (i + 1) * lanes
                ]
    for i in range(blocks):
        returned[:, i * lanes : (i + 1) * lanes] = wide[i].astype(jnp.bfloat16)


def couple_kernel(own, other, own_matrix, other_matrix, weight, sent):
    total = jnp.dot(own[...], own_matrix[...], preferred_element_type=jnp.float32)
    total += jnp.dot(other[...], other_matrix[...], preferred_element_type=jnp.float32)
    total *= weight[...]
    blocks, rows, lanes = sent.shape
    for i in range(blocks):
        sent[i] = total[:, i * lanes : (i + 1) * lanes].astype(jnp.bfloat16)


def call(kernel, out_shape, flops, limit, *operands, scratch=()):
    moved = sum(x.size * x.dtype.itemsize for x in operands) + out_shape.size * 2
    return pl.pallas_call(
        kernel,
        out_shape=out_shape,
        in_specs=[pl.BlockSpec(memory_space=pltpu.VMEM)] * len(operands),
        out_specs=pl.BlockSpec(memory_space=pltpu.VMEM),
        scratch_shapes=scratch,
        compiler_params=pltpu.CompilerParams(vmem_limit_bytes=limit << 20),
        cost_estimate=pl.CostEstimate(flops=flops, bytes_accessed=moved, transcendentals=0),
    )(*operands)


def local(spectral, legendre, pattern, assignment, quad_weight, coupling):
    degrees = spectral.shape[1]
    channels = spectral.shape[3]
    lat_count = legendre.shape[1]
    wave_total = assignment.shape[0]
    y_count = SIZES["y"]
    peers = y_count * wave_total
    lats = lat_count // peers
    rows = wave_total * lats * 2
    own_levels = channels // F
    slot = lax.axis_index("z") * SIZES["x"] + lax.axis_index("x")
    core = lax.axis_index("core")

    own_wave = lax.dynamic_index_in_dim(assignment, slot, 0, keepdims=False)
    own_mask = lax.dynamic_index_in_dim(pattern, own_wave, 0, keepdims=False).astype(jnp.bfloat16)
    lat_tiles, deg_tiles = own_mask.shape
    wide_mask = jnp.broadcast_to(
        own_mask[:, None, :, None], (lat_tiles, TILE, deg_tiles, TILE)
    ).reshape(lat_count, degrees)
    pruned = legendre[0] * wide_mask

    at_lats = forward(spectral[0], legendre[0], pattern, assignment)
    at_lats = at_lats.reshape(peers, lats, 2, channels)
    received = lax.all_to_all(at_lats, PEERS, split_axis=0, concat_axis=0, tiled=True)
    received = received.reshape(y_count, rows, channels)

    arrival = assignment.reshape(SIZES["z"], SIZES["x"]).T.reshape(wave_total)
    lon_count = 3 * wave_total
    synthesis, analysis = wave_tables(arrival, lon_count)
    cores = SIZES["core"]
    split = coupling.reshape(y_count, cores, own_levels, y_count, cores, own_levels)
    mine = lax.dynamic_index_in_dim(split, core, 1, keepdims=False)
    wide = y_count * channels
    spread = (
        jnp.arange(wide, dtype=jnp.int32)[:, None] // F
        == jnp.arange(wide // F, dtype=jnp.int32)[None, :]
    ).astype(jnp.bfloat16)
    same_field = (
        jnp.arange(wide, dtype=jnp.int32)[:, None] % F
        == jnp.arange(wide, dtype=jnp.int32)[None, :] % F
    )

    def matrix(source):
        small = lax.dynamic_index_in_dim(mine, source, 3, keepdims=False)
        small = small.reshape(wide // F, wide // F)
        tall = jnp.einsum("pb,ab->pa", spread, small).astype(jnp.bfloat16)
        full = jnp.einsum("pa,qa->pq", tall, spread).astype(jnp.bfloat16)
        return jnp.where(same_field, full, jnp.zeros((), jnp.bfloat16))

    group = lax.axis_index(PEERS)
    weight = lax.dynamic_slice_in_dim(quad_weight, group * lats, lats)
    weight = jnp.broadcast_to(weight[None, :, None], (wave_total, lats, 2)).reshape(rows, 1)
    own_matrix, other_matrix = matrix(core), matrix(1 - core)
    received, synthesis, analysis, own_matrix, other_matrix, weight, pruned = (
        lax.optimization_barrier(
            (received, synthesis, analysis, own_matrix, other_matrix, weight, pruned)
        )
    )

    wide = y_count * channels
    flops = 4 * lon_count * rows * wide
    returned = call(
        functools.partial(grid_kernel, lats),
        jax.ShapeDtypeStruct((rows, wide), jnp.bfloat16),
        flops,
        16,
        received,
        synthesis,
        analysis,
        scratch=[pltpu.VMEM((y_count, rows, channels), jnp.float32)] * 2,
    )
    swapped = lax.ppermute(returned, "core", [(0, 1), (1, 0)])

    sent = call(
        couple_kernel,
        jax.ShapeDtypeStruct((y_count, rows, channels), jnp.bfloat16),
        4 * rows * wide * wide,
        16,
        returned,
        swapped,
        own_matrix,
        other_matrix,
        weight,
    )
    sent = sent.reshape(peers, lats, 2, channels)
    weighted = lax.all_to_all(sent, PEERS, split_axis=0, concat_axis=0, tiled=True)
    weighted = weighted.reshape(lat_count, 2, channels)
    tendency = jnp.einsum("ln,lch->nch", pruned, weighted, preferred_element_type=jnp.float32)
    return tendency.astype(jnp.bfloat16)[None]


def solution(mesh):
    grid = Mesh(mesh.devices.reshape(tuple(SIZES.values())), tuple(SIZES))
    wave, lev = ("z", "x"), ("y", "core")
    placed = (P(wave, None, None, lev), P(wave, None, None), P(), P(), P(), P())
    return jax.shard_map(
        local,
        mesh=grid,
        in_specs=placed,
        out_specs=P(wave, None, None, lev),
        check_vma=False,
    )
```

```python
import functools
import math

import jax
import jax.numpy as jnp
from jax import lax
from jax.experimental import pallas as pl
from jax.experimental.pallas import tpu as pltpu
from jax.sharding import Mesh
from jax.sharding import PartitionSpec as P

F = 8
TILE = 128
LAT_CHUNKS = 2
PEERS = ("y", "x", "z")
SIZES = {"z": 16, "x": 4, "y": 4, "core": 2}


def middle(axis):
    return SIZES[axis] // 2


def peer_groups():
    order = [
        [(place + middle(axis)) % SIZES[axis] for place in range(SIZES[axis])] for axis in PEERS
    ]
    return [
        [
            ((z * SIZES["x"] + x) * SIZES["y"] + y) * SIZES["core"] + core
            for y in order[0]
            for x in order[1]
            for z in order[2]
        ]
        for core in range(SIZES["core"])
    ]


def own_position():
    position = 0
    for axis in PEERS:
        place = lax.rem(lax.axis_index(axis) + middle(axis), SIZES[axis])
        position = position * SIZES[axis] + place
    return position


def exchange(values):
    return lax.all_to_all(
        values,
        tuple(SIZES),
        split_axis=0,
        concat_axis=0,
        axis_index_groups=peer_groups(),
        tiled=True,
    )


def wave_tables(waves, lon_count):
    wave_total = waves.shape[0]
    longitudes = jnp.arange(lon_count, dtype=jnp.int32)
    phases = longitudes[:, None] * waves[None, :] % lon_count
    angles = phases.astype(jnp.float32) * (2.0 * math.pi / lon_count)
    basis = jnp.concatenate([jnp.cos(angles), -jnp.sin(angles)], axis=1)
    synthesis = (basis / math.sqrt(wave_total)).astype(jnp.bfloat16)
    analysis = (basis.T / math.sqrt(lon_count)).astype(jnp.bfloat16)
    return synthesis, analysis


def forward_kernel(
    spectral, legendre, pattern, assignment, at_lats,
    raw, matrix, blocks, waves, paired, coeffs, wide, merged, in_sem, lat_sem, out_sem,
):
    lat_tiles, deg_tiles, _ = pattern.shape
    lat_count, degrees = legendre.shape
    lanes = raw.shape[1]
    chunk = lat_count // LAT_CHUNKS
    copies = [
        pltpu.make_async_copy(source, target, in_sem.at[i])
        for i, (source, target) in enumerate(
            ((spectral, raw), (assignment, waves), (pattern, blocks))
        )
    ]
    for copy in copies:
        copy.start()

    def lat_copy(i):
        span = pl.ds(i * chunk, chunk)
        return pltpu.make_async_copy(legendre.at[span], matrix.at[span], lat_sem.at[i])

    def out_copy(i):
        span = pl.ds(2 * i * chunk, 2 * chunk)
        return pltpu.make_async_copy(merged.at[span], at_lats.at[span], out_sem.at[i])

    for i in range(LAT_CHUNKS):
        lat_copy(i).start()
    copies[0].wait()
    paired[...] = raw[...].astype(jnp.float32)
    for part in range(2):
        coeffs[:, part * lanes : (part + 1) * lanes] = paired[
            pl.ds(part, degrees, stride=2), :
        ].astype(jnp.bfloat16)
    copies[1].wait()
    copies[2].wait()
    slot = lax.axis_index("z") * SIZES["x"] + lax.axis_index("x")
    wave = waves[slot]
    picked = lax.broadcasted_iota(jnp.int32, blocks.shape, 2) == wave
    mask = jnp.sum(jnp.where(picked, blocks[...], 0), axis=2, keepdims=True)
    for i in range(LAT_CHUNKS):
        lat_copy(i).wait()
        for t in range(i * lat_tiles // LAT_CHUNKS, (i + 1) * lat_tiles // LAT_CHUNKS):
            keep = jnp.concatenate(
                [
                    jnp.broadcast_to(mask[t, k : k + 1, :], (TILE, TILE)).astype(jnp.bfloat16)
                    for k in range(deg_tiles)
                ],
                axis=1,
            )
            tile = slice(TILE * t, TILE * (t + 1))
            matrix[tile, :] = matrix[tile, :] * keep
        found = jnp.dot(
            matrix[chunk * i : chunk * (i + 1), :],
            coeffs[...],
            preferred_element_type=jnp.float32,
        )
        for part in range(2):
            wide[pl.ds(part, chunk, stride=2), :] = found[:, part * lanes : (part + 1) * lanes]
        merged[2 * chunk * i : 2 * chunk * (i + 1), :] = wide[...].astype(jnp.bfloat16)
        out_copy(i).start()
    for i in range(LAT_CHUNKS):
        out_copy(i).wait()


def forward(spectral, legendre, pattern, assignment):
    degrees, _, channels = spectral.shape
    lat_count = legendre.shape[0]
    pattern = jnp.transpose(pattern, (1, 2, 0))
    chunk = lat_count // LAT_CHUNKS
    return pl.pallas_call(
        forward_kernel,
        out_shape=jax.ShapeDtypeStruct((2 * lat_count, channels), jnp.bfloat16),
        in_specs=[pl.BlockSpec(memory_space=pltpu.HBM)] * 4,
        out_specs=pl.BlockSpec(memory_space=pltpu.HBM),
        scratch_shapes=[
            pltpu.VMEM((2 * degrees, channels), jnp.bfloat16),
            pltpu.VMEM((lat_count, degrees), jnp.bfloat16),
            pltpu.VMEM(pattern.shape, jnp.int32),
            pltpu.SMEM(assignment.shape, jnp.int32),
            pltpu.VMEM((2 * degrees, channels), jnp.float32),
            pltpu.VMEM((degrees, 2 * channels), jnp.bfloat16),
            pltpu.VMEM((2 * chunk, channels), jnp.float32),
            pltpu.VMEM((2 * lat_count, channels), jnp.bfloat16),
            pltpu.SemaphoreType.DMA((3,)),
            pltpu.SemaphoreType.DMA((LAT_CHUNKS,)),
            pltpu.SemaphoreType.DMA((LAT_CHUNKS,)),
        ],
    )(spectral.reshape(2 * degrees, channels), legendre, pattern, assignment)


def grid_kernel(lats, received, synthesis, analysis, returned, wide, ahead):
    blocks, rows, lanes = received.shape
    width = blocks * lanes
    slots = rows // (2 * lats)
    wide[...] = received[...].astype(jnp.float32)
    pair = 2 * lanes
    source = lax.broadcasted_iota(jnp.int32, (pair, pair), 0)
    target = lax.broadcasted_iota(jnp.int32, (pair, pair), 1)
    advance = (source == target // F * F + (target + 1) % F).astype(jnp.bfloat16)
    for i in range(0, blocks, 2):
        both = jnp.concatenate([received[i], received[i + 1]], axis=1)
        moved = jnp.dot(both, advance, preferred_element_type=jnp.float32)
        ahead[i] = moved[:, :lanes]
        ahead[i + 1] = moved[:, lanes:]

    def span(lat, part):
        return pl.ds(2 * lat + part, slots, stride=2 * lats)

    def gather(rows_of, lat):
        parts = [
            jnp.concatenate([rows_of[i, span(lat, part), :] for i in range(blocks)], axis=1)
            for part in range(2)
        ]
        return jnp.concatenate(parts, axis=0).astype(jnp.bfloat16)

    for lat in range(lats):
        field, partner = (
            jnp.dot(synthesis[...], gather(rows_of, lat), preferred_element_type=jnp.float32)
            for rows_of in (wide, ahead)
        )
        product = (field * partner).astype(jnp.bfloat16)
        back = jnp.dot(analysis[...], product, preferred_element_type=jnp.float32)
        for part in range(2):
            for i in range(blocks):
                wide[i, span(lat, part), :] = back[
                    part * slots : (part + 1) * slots, i * lanes : (i + 1) * lanes
                ]
    for i in range(blocks):
        returned[:, i * lanes : (i + 1) * lanes] = wide[i].astype(jnp.bfloat16)


def couple_kernel(own, other, own_matrix, other_matrix, weight, sent):
    total = jnp.dot(own[...], own_matrix[...], preferred_element_type=jnp.float32)
    total += jnp.dot(other[...], other_matrix[...], preferred_element_type=jnp.float32)
    total *= weight[...]
    blocks, rows, lanes = sent.shape
    for i in range(blocks):
        sent[i] = total[:, i * lanes : (i + 1) * lanes].astype(jnp.bfloat16)


def call(kernel, out_shape, flops, limit, *operands, scratch=()):
    moved = sum(x.size * x.dtype.itemsize for x in operands) + out_shape.size * 2
    return pl.pallas_call(
        kernel,
        out_shape=out_shape,
        in_specs=[pl.BlockSpec(memory_space=pltpu.VMEM)] * len(operands),
        out_specs=pl.BlockSpec(memory_space=pltpu.VMEM),
        scratch_shapes=scratch,
        compiler_params=pltpu.CompilerParams(vmem_limit_bytes=limit << 20),
        cost_estimate=pl.CostEstimate(flops=flops, bytes_accessed=moved, transcendentals=0),
    )(*operands)


def local(spectral, legendre, pattern, assignment, quad_weight, coupling):
    degrees = spectral.shape[1]
    channels = spectral.shape[3]
    lat_count = legendre.shape[1]
    wave_total = assignment.shape[0]
    y_count = SIZES["y"]
    peers = y_count * wave_total
    lats = lat_count // peers
    rows = wave_total * lats * 2
    own_levels = channels // F
    slot = lax.axis_index("z") * SIZES["x"] + lax.axis_index("x")
    core = lax.axis_index("core")

    own_wave = lax.dynamic_index_in_dim(assignment, slot, 0, keepdims=False)
    own_mask = lax.dynamic_index_in_dim(pattern, own_wave, 0, keepdims=False).astype(jnp.bfloat16)
    lat_tiles, deg_tiles = own_mask.shape
    wide_mask = jnp.broadcast_to(
        own_mask[:, None, :, None], (lat_tiles, TILE, deg_tiles, TILE)
    ).reshape(lat_count, degrees)
    pruned = legendre[0] * wide_mask

    at_lats = forward(spectral[0], legendre[0], pattern, assignment)
    at_lats = at_lats.reshape(peers, lats, 2, channels)
    received = exchange(at_lats)
    received = received.reshape(y_count, rows, channels)

    arrival = assignment.reshape(SIZES["z"], SIZES["x"])
    arrival = jnp.roll(arrival, (-middle("z"), -middle("x")), (0, 1)).T.reshape(wave_total)
    lon_count = 3 * wave_total
    synthesis, analysis = wave_tables(arrival, lon_count)
    cores = SIZES["core"]
    split = coupling.reshape(y_count, cores, own_levels, y_count, cores, own_levels)
    split = jnp.roll(split, (-middle("y"), -middle("y")), (0, 3))
    mine = lax.dynamic_index_in_dim(split, core, 1, keepdims=False)
    wide = y_count * channels
    spread = (
        jnp.arange(wide, dtype=jnp.int32)[:, None] // F
        == jnp.arange(wide // F, dtype=jnp.int32)[None, :]
    ).astype(jnp.bfloat16)
    same_field = (
        jnp.arange(wide, dtype=jnp.int32)[:, None] % F
        == jnp.arange(wide, dtype=jnp.int32)[None, :] % F
    )

    def matrix(source):
        small = lax.dynamic_index_in_dim(mine, source, 3, keepdims=False)
        small = small.reshape(wide // F, wide // F)
        tall = jnp.einsum("pb,ab->pa", spread, small).astype(jnp.bfloat16)
        full = jnp.einsum("pa,qa->pq", tall, spread).astype(jnp.bfloat16)
        return jnp.where(same_field, full, jnp.zeros((), jnp.bfloat16))

    group = own_position()
    weight = lax.dynamic_slice_in_dim(quad_weight, group * lats, lats)
    weight = jnp.broadcast_to(weight[None, :, None], (wave_total, lats, 2)).reshape(rows, 1)
    own_matrix, other_matrix = matrix(core), matrix(1 - core)
    received, synthesis, analysis, own_matrix, other_matrix, weight, pruned = (
        lax.optimization_barrier(
            (received, synthesis, analysis, own_matrix, other_matrix, weight, pruned)
        )
    )

    wide = y_count * channels
    flops = 4 * lon_count * rows * wide
    returned = call(
        functools.partial(grid_kernel, lats),
        jax.ShapeDtypeStruct((rows, wide), jnp.bfloat16),
        flops,
        16,
        received,
        synthesis,
        analysis,
        scratch=[pltpu.VMEM((y_count, rows, channels), jnp.float32)] * 2,
    )
    swapped = lax.ppermute(returned, "core", [(0, 1), (1, 0)])

    sent = call(
        couple_kernel,
        jax.ShapeDtypeStruct((y_count, rows, channels), jnp.bfloat16),
        4 * rows * wide * wide,
        16,
        returned,
        swapped,
        own_matrix,
        other_matrix,
        weight,
    )
    sent = sent.reshape(peers, lats, 2, channels)
    weighted = exchange(sent)
    weighted = weighted.reshape(lat_count, 2, channels)
    tendency = jnp.einsum("ln,lch->nch", pruned, weighted, preferred_element_type=jnp.float32)
    return tendency.astype(jnp.bfloat16)[None]


def solution(mesh):
    grid = Mesh(mesh.devices.reshape(tuple(SIZES.values())), tuple(SIZES))
    wave, lev = ("z", "x"), ("y", "core")
    placed = (P(wave, None, None, lev), P(wave, None, None), P(), P(), P(), P())
    return jax.shard_map(
        local,
        mesh=grid,
        in_specs=placed,
        out_specs=P(wave, None, None, lev),
        check_vma=False,
    )
```

```python
import functools
import math

import jax
import jax.numpy as jnp
from jax import lax
from jax.experimental import pallas as pl
from jax.experimental.pallas import tpu as pltpu
from jax.sharding import Mesh
from jax.sharding import PartitionSpec as P

F = 8
TILE = 128
LAT_CHUNKS = 2
LAT_PARTS = 2
PEERS = ("y", "x", "z")
SIZES = {"z": 16, "x": 4, "y": 4, "core": 2}


def middle(axis):
    return SIZES[axis] // 2


def peer_groups():
    order = [
        [(place + middle(axis)) % SIZES[axis] for place in range(SIZES[axis])] for axis in PEERS
    ]
    return [
        [
            ((z * SIZES["x"] + x) * SIZES["y"] + y) * SIZES["core"] + core
            for y in order[0]
            for x in order[1]
            for z in order[2]
        ]
        for core in range(SIZES["core"])
    ]


def own_position():
    position = 0
    for axis in PEERS:
        place = lax.rem(lax.axis_index(axis) + middle(axis), SIZES[axis])
        position = position * SIZES[axis] + place
    return position


def exchange(values):
    return lax.all_to_all(
        values,
        tuple(SIZES),
        split_axis=0,
        concat_axis=0,
        axis_index_groups=peer_groups(),
        tiled=True,
    )


def wave_tables(waves, lon_count):
    wave_total = waves.shape[0]
    longitudes = jnp.arange(lon_count, dtype=jnp.int32)
    phases = longitudes[:, None] * waves[None, :] % lon_count
    angles = phases.astype(jnp.float32) * (2.0 * math.pi / lon_count)
    basis = jnp.concatenate([jnp.cos(angles), -jnp.sin(angles)], axis=1)
    synthesis = (basis / math.sqrt(wave_total)).astype(jnp.bfloat16)
    analysis = (basis.T / math.sqrt(lon_count)).astype(jnp.bfloat16)
    return synthesis, analysis


def forward_kernel(
    spectral, legendre, pattern, assignment, at_lats,
    raw, matrix, blocks, waves, paired, coeffs, wide, merged, in_sem, lat_sem, out_sem,
):
    lat_tiles, deg_tiles, _ = pattern.shape
    lat_count, degrees = legendre.shape
    lanes = raw.shape[1]
    chunk = lat_count // LAT_CHUNKS
    copies = [
        pltpu.make_async_copy(source, target, in_sem.at[i])
        for i, (source, target) in enumerate(
            ((spectral, raw), (assignment, waves), (pattern, blocks))
        )
    ]
    for copy in copies:
        copy.start()

    def lat_copy(i):
        span = pl.ds(i * chunk, chunk)
        return pltpu.make_async_copy(legendre.at[span], matrix.at[span], lat_sem.at[i])

    def out_copy(i):
        span = pl.ds(2 * i * chunk, 2 * chunk)
        return pltpu.make_async_copy(merged.at[span], at_lats.at[span], out_sem.at[i])

    for i in range(LAT_CHUNKS):
        lat_copy(i).start()
    copies[0].wait()
    paired[...] = raw[...].astype(jnp.float32)
    for part in range(2):
        coeffs[:, part * lanes : (part + 1) * lanes] = paired[
            pl.ds(part, degrees, stride=2), :
        ].astype(jnp.bfloat16)
    copies[1].wait()
    copies[2].wait()
    slot = lax.axis_index("z") * SIZES["x"] + lax.axis_index("x")
    wave = waves[slot]
    picked = lax.broadcasted_iota(jnp.int32, blocks.shape, 2) == wave
    mask = jnp.sum(jnp.where(picked, blocks[...], 0), axis=2, keepdims=True)
    for i in range(LAT_CHUNKS):
        lat_copy(i).wait()
        for t in range(i * lat_tiles // LAT_CHUNKS, (i + 1) * lat_tiles // LAT_CHUNKS):
            keep = jnp.concatenate(
                [
                    jnp.broadcast_to(mask[t, k : k + 1, :], (TILE, TILE)).astype(jnp.bfloat16)
                    for k in range(deg_tiles)
                ],
                axis=1,
            )
            tile = slice(TILE * t, TILE * (t + 1))
            matrix[tile, :] = matrix[tile, :] * keep
        depth = chunk // LAT_PARTS
        founds = [
            jnp.dot(
                matrix[pl.ds(chunk * i + depth * j, depth), :],
                coeffs[...],
                preferred_element_type=jnp.float32,
            )
            for j in range(LAT_PARTS)
        ]
        for j, found in enumerate(founds):
            for part in range(2):
                wide[pl.ds(2 * depth * j + part, depth, stride=2), :] = found[
                    :, part * lanes : (part + 1) * lanes
                ]
        merged[2 * chunk * i : 2 * chunk * (i + 1), :] = wide[...].astype(jnp.bfloat16)
        out_copy(i).start()
    for i in range(LAT_CHUNKS):
        out_copy(i).wait()


def forward(spectral, legendre, pattern, assignment):
    degrees, _, channels = spectral.shape
    lat_count = legendre.shape[0]
    pattern = jnp.transpose(pattern, (1, 2, 0))
    chunk = lat_count // LAT_CHUNKS
    return pl.pallas_call(
        forward_kernel,
        out_shape=jax.ShapeDtypeStruct((2 * lat_count, channels), jnp.bfloat16),
        in_specs=[pl.BlockSpec(memory_space=pltpu.HBM)] * 4,
        out_specs=pl.BlockSpec(memory_space=pltpu.HBM),
        scratch_shapes=[
            pltpu.VMEM((2 * degrees, channels), jnp.bfloat16),
            pltpu.VMEM((lat_count, degrees), jnp.bfloat16),
            pltpu.VMEM(pattern.shape, jnp.int32),
            pltpu.SMEM(assignment.shape, jnp.int32),
            pltpu.VMEM((2 * degrees, channels), jnp.float32),
            pltpu.VMEM((degrees, 2 * channels), jnp.bfloat16),
            pltpu.VMEM((2 * chunk, channels), jnp.float32),
            pltpu.VMEM((2 * lat_count, channels), jnp.bfloat16),
            pltpu.SemaphoreType.DMA((3,)),
            pltpu.SemaphoreType.DMA((LAT_CHUNKS,)),
            pltpu.SemaphoreType.DMA((LAT_CHUNKS,)),
        ],
    )(spectral.reshape(2 * degrees, channels), legendre, pattern, assignment)


def grid_kernel(lats, received, synthesis, analysis, returned, wide, ahead, back_rows, products):
    blocks, rows, lanes = received.shape
    width = blocks * lanes
    slots = rows // (2 * lats)
    wide[...] = received[...].astype(jnp.float32)
    pair = 2 * lanes
    source = lax.broadcasted_iota(jnp.int32, (pair, pair), 0)
    target = lax.broadcasted_iota(jnp.int32, (pair, pair), 1)
    advance = (source == target // F * F + (target + 1) % F).astype(jnp.bfloat16)
    for i in range(0, blocks, 2):
        both = jnp.concatenate([received[i], received[i + 1]], axis=1)
        moved = jnp.dot(both, advance, preferred_element_type=jnp.float32)
        ahead[i] = moved[:, :lanes]
        ahead[i + 1] = moved[:, lanes:]

    def span(lat, part):
        return pl.ds(2 * lat + part, slots, stride=2 * lats)

    def gather(rows_of, lat):
        parts = [
            jnp.concatenate([rows_of[i, span(lat, part), :] for i in range(blocks)], axis=1)
            for part in range(2)
        ]
        return jnp.concatenate(parts, axis=0).astype(jnp.bfloat16)

    for lat in range(lats):
        field, partner = (
            jnp.dot(synthesis[...], gather(rows_of, lat), preferred_element_type=jnp.float32)
            for rows_of in (wide, ahead)
        )
        products[lat] = (field * partner).astype(jnp.bfloat16)
    for lat in range(lats):
        back = jnp.dot(analysis[...], products[lat], preferred_element_type=jnp.float32)
        for part in range(2):
            for i in range(blocks):
                back_rows[i, span(lat, part), :] = back[
                    part * slots : (part + 1) * slots, i * lanes : (i + 1) * lanes
                ]
    for i in range(blocks):
        returned[:, i * lanes : (i + 1) * lanes] = back_rows[i].astype(jnp.bfloat16)


def couple_kernel(own, other, own_matrix, other_matrix, weight, sent):
    total = jnp.dot(own[...], own_matrix[...], preferred_element_type=jnp.float32)
    total += jnp.dot(other[...], other_matrix[...], preferred_element_type=jnp.float32)
    total *= weight[...]
    blocks, rows, lanes = sent.shape
    for i in range(blocks):
        sent[i] = total[:, i * lanes : (i + 1) * lanes].astype(jnp.bfloat16)


def call(kernel, out_shape, flops, limit, *operands, scratch=()):
    moved = sum(x.size * x.dtype.itemsize for x in operands) + out_shape.size * 2
    return pl.pallas_call(
        kernel,
        out_shape=out_shape,
        in_specs=[pl.BlockSpec(memory_space=pltpu.VMEM)] * len(operands),
        out_specs=pl.BlockSpec(memory_space=pltpu.VMEM),
        scratch_shapes=scratch,
        compiler_params=pltpu.CompilerParams(vmem_limit_bytes=limit << 20),
        cost_estimate=pl.CostEstimate(flops=flops, bytes_accessed=moved, transcendentals=0),
    )(*operands)


def local(spectral, legendre, pattern, assignment, quad_weight, coupling):
    degrees = spectral.shape[1]
    channels = spectral.shape[3]
    lat_count = legendre.shape[1]
    wave_total = assignment.shape[0]
    y_count = SIZES["y"]
    peers = y_count * wave_total
    lats = lat_count // peers
    rows = wave_total * lats * 2
    own_levels = channels // F
    slot = lax.axis_index("z") * SIZES["x"] + lax.axis_index("x")
    core = lax.axis_index("core")

    own_wave = lax.dynamic_index_in_dim(assignment, slot, 0, keepdims=False)
    own_mask = lax.dynamic_index_in_dim(pattern, own_wave, 0, keepdims=False).astype(jnp.bfloat16)
    lat_tiles, deg_tiles = own_mask.shape
    wide_mask = jnp.broadcast_to(
        own_mask[:, None, :, None], (lat_tiles, TILE, deg_tiles, TILE)
    ).reshape(lat_count, degrees)
    pruned = legendre[0] * wide_mask

    at_lats = forward(spectral[0], legendre[0], pattern, assignment)
    at_lats = at_lats.reshape(peers, lats, 2, channels)
    received = exchange(at_lats)
    received = received.reshape(y_count, rows, channels)

    arrival = assignment.reshape(SIZES["z"], SIZES["x"])
    arrival = jnp.roll(arrival, (-middle("z"), -middle("x")), (0, 1)).T.reshape(wave_total)
    lon_count = 3 * wave_total
    synthesis, analysis = wave_tables(arrival, lon_count)
    cores = SIZES["core"]
    split = coupling.reshape(y_count, cores, own_levels, y_count, cores, own_levels)
    split = jnp.roll(split, (-middle("y"), -middle("y")), (0, 3))
    mine = lax.dynamic_index_in_dim(split, core, 1, keepdims=False)
    wide = y_count * channels
    spread = (
        jnp.arange(wide, dtype=jnp.int32)[:, None] // F
        == jnp.arange(wide // F, dtype=jnp.int32)[None, :]
    ).astype(jnp.bfloat16)
    same_field = (
        jnp.arange(wide, dtype=jnp.int32)[:, None] % F
        == jnp.arange(wide, dtype=jnp.int32)[None, :] % F
    )

    def matrix(source):
        small = lax.dynamic_index_in_dim(mine, source, 3, keepdims=False)
        small = small.reshape(wide // F, wide // F)
        tall = jnp.einsum("pb,ab->pa", spread, small).astype(jnp.bfloat16)
        full = jnp.einsum("pa,qa->pq", tall, spread).astype(jnp.bfloat16)
        return jnp.where(same_field, full, jnp.zeros((), jnp.bfloat16))

    group = own_position()
    weight = lax.dynamic_slice_in_dim(quad_weight, group * lats, lats)
    weight = jnp.broadcast_to(weight[None, :, None], (wave_total, lats, 2)).reshape(rows, 1)
    own_matrix, other_matrix = matrix(core), matrix(1 - core)
    received, synthesis, analysis, own_matrix, other_matrix, weight, pruned = (
        lax.optimization_barrier(
            (received, synthesis, analysis, own_matrix, other_matrix, weight, pruned)
        )
    )

    wide = y_count * channels
    flops = 4 * lon_count * rows * wide
    returned = call(
        functools.partial(grid_kernel, lats),
        jax.ShapeDtypeStruct((rows, wide), jnp.bfloat16),
        flops,
        16,
        received,
        synthesis,
        analysis,
        scratch=[pltpu.VMEM((y_count, rows, channels), jnp.float32)] * 3
        + [pltpu.VMEM((lats, lon_count, wide), jnp.bfloat16)],
    )
    swapped = lax.ppermute(returned, "core", [(0, 1), (1, 0)])

    sent = call(
        couple_kernel,
        jax.ShapeDtypeStruct((y_count, rows, channels), jnp.bfloat16),
        4 * rows * wide * wide,
        16,
        returned,
        swapped,
        own_matrix,
        other_matrix,
        weight,
    )
    sent = sent.reshape(peers, lats, 2, channels)
    weighted = exchange(sent)
    weighted = weighted.reshape(lat_count, 2, channels)
    tendency = jnp.einsum("ln,lch->nch", pruned, weighted, preferred_element_type=jnp.float32)
    return tendency.astype(jnp.bfloat16)[None]


def solution(mesh):
    grid = Mesh(mesh.devices.reshape(tuple(SIZES.values())), tuple(SIZES))
    wave, lev = ("z", "x"), ("y", "core")
    placed = (P(wave, None, None, lev), P(wave, None, None), P(), P(), P(), P())
    return jax.shard_map(
        local,
        mesh=grid,
        in_specs=placed,
        out_specs=P(wave, None, None, lev),
        check_vma=False,
    )
```

```python
import functools
import math

import jax
import jax.numpy as jnp
from jax import lax
from jax.experimental import pallas as pl
from jax.experimental.pallas import tpu as pltpu
from jax.sharding import Mesh
from jax.sharding import PartitionSpec as P

F = 8
TILE = 128
LAT_CHUNKS = 2
LAT_PARTS = 2
PEERS = ("y", "x", "z")
SIZES = {"z": 16, "x": 4, "y": 4, "core": 2}


def middle(axis):
    return SIZES[axis] // 2


def peer_groups():
    order = [
        [(place + middle(axis)) % SIZES[axis] for place in range(SIZES[axis])] for axis in PEERS
    ]
    return [
        [
            ((z * SIZES["x"] + x) * SIZES["y"] + y) * SIZES["core"] + core
            for y in order[0]
            for x in order[1]
            for z in order[2]
        ]
        for core in range(SIZES["core"])
    ]


def own_position():
    position = 0
    for axis in PEERS:
        place = lax.rem(lax.axis_index(axis) + middle(axis), SIZES[axis])
        position = position * SIZES[axis] + place
    return position


def exchange(values):
    return lax.all_to_all(
        values,
        tuple(SIZES),
        split_axis=0,
        concat_axis=0,
        axis_index_groups=peer_groups(),
        tiled=True,
    )


def wave_tables(waves, lon_count):
    wave_total = waves.shape[0]
    longitudes = jnp.arange(lon_count, dtype=jnp.int32)
    phases = longitudes[:, None] * waves[None, :] % lon_count
    angles = phases.astype(jnp.float32) * (2.0 * math.pi / lon_count)
    basis = jnp.concatenate([jnp.cos(angles), -jnp.sin(angles)], axis=1)
    synthesis = (basis / math.sqrt(wave_total)).astype(jnp.bfloat16)
    analysis = (basis.T / math.sqrt(lon_count)).astype(jnp.bfloat16)
    return synthesis, analysis


def forward_kernel(
    spectral, legendre, pattern, assignment, at_lats,
    raw, matrix, blocks, waves, paired, coeffs, wide, merged, in_sem, lat_sem, out_sem,
):
    lat_tiles, deg_tiles, _ = pattern.shape
    lat_count, degrees = legendre.shape
    lanes = raw.shape[1]
    chunk = lat_count // LAT_CHUNKS
    copies = [
        pltpu.make_async_copy(source, target, in_sem.at[i])
        for i, (source, target) in enumerate(
            ((spectral, raw), (assignment, waves), (pattern, blocks))
        )
    ]
    for copy in copies:
        copy.start()

    def lat_copy(i):
        span = pl.ds(i * chunk, chunk)
        return pltpu.make_async_copy(legendre.at[span], matrix.at[span], lat_sem.at[i])

    def out_copy(i):
        span = pl.ds(2 * i * chunk, 2 * chunk)
        return pltpu.make_async_copy(merged.at[span], at_lats.at[span], out_sem.at[i])

    for i in range(LAT_CHUNKS):
        lat_copy(i).start()
    copies[0].wait()
    paired[...] = raw[...].astype(jnp.float32)
    for part in range(2):
        coeffs[:, part * lanes : (part + 1) * lanes] = paired[
            pl.ds(part, degrees, stride=2), :
        ].astype(jnp.bfloat16)
    copies[1].wait()
    copies[2].wait()
    slot = lax.axis_index("z") * SIZES["x"] + lax.axis_index("x")
    wave = waves[slot]
    picked = lax.broadcasted_iota(jnp.int32, blocks.shape, 2) == wave
    mask = jnp.sum(jnp.where(picked, blocks[...], 0), axis=2, keepdims=True)
    for i in range(LAT_CHUNKS):
        lat_copy(i).wait()
        for t in range(i * lat_tiles // LAT_CHUNKS, (i + 1) * lat_tiles // LAT_CHUNKS):
            keep = jnp.concatenate(
                [
                    jnp.broadcast_to(mask[t, k : k + 1, :], (TILE, TILE)).astype(jnp.bfloat16)
                    for k in range(deg_tiles)
                ],
                axis=1,
            )
            tile = slice(TILE * t, TILE * (t + 1))
            matrix[tile, :] = matrix[tile, :] * keep
        depth = chunk // LAT_PARTS
        founds = [
            jnp.dot(
                matrix[pl.ds(chunk * i + depth * j, depth), :],
                coeffs[...],
                preferred_element_type=jnp.float32,
            )
            for j in range(LAT_PARTS)
        ]
        for j, found in enumerate(founds):
            for part in range(2):
                wide[pl.ds(2 * depth * j + part, depth, stride=2), :] = found[
                    :, part * lanes : (part + 1) * lanes
                ]
        merged[2 * chunk * i : 2 * chunk * (i + 1), :] = wide[...].astype(jnp.bfloat16)
        out_copy(i).start()
    for i in range(LAT_CHUNKS):
        out_copy(i).wait()


def forward(spectral, legendre, pattern, assignment):
    degrees, _, channels = spectral.shape
    lat_count = legendre.shape[0]
    pattern = jnp.transpose(pattern, (1, 2, 0))
    chunk = lat_count // LAT_CHUNKS
    return pl.pallas_call(
        forward_kernel,
        out_shape=jax.ShapeDtypeStruct((2 * lat_count, channels), jnp.bfloat16),
        in_specs=[pl.BlockSpec(memory_space=pltpu.HBM)] * 4,
        out_specs=pl.BlockSpec(memory_space=pltpu.HBM),
        scratch_shapes=[
            pltpu.VMEM((2 * degrees, channels), jnp.bfloat16),
            pltpu.VMEM((lat_count, degrees), jnp.bfloat16),
            pltpu.VMEM(pattern.shape, jnp.int32),
            pltpu.SMEM(assignment.shape, jnp.int32),
            pltpu.VMEM((2 * degrees, channels), jnp.float32),
            pltpu.VMEM((degrees, 2 * channels), jnp.bfloat16),
            pltpu.VMEM((2 * chunk, channels), jnp.float32),
            pltpu.VMEM((2 * lat_count, channels), jnp.bfloat16),
            pltpu.SemaphoreType.DMA((3,)),
            pltpu.SemaphoreType.DMA((LAT_CHUNKS,)),
            pltpu.SemaphoreType.DMA((LAT_CHUNKS,)),
        ],
    )(spectral.reshape(2 * degrees, channels), legendre, pattern, assignment)


def grid_kernel(lats, received, synthesis, analysis, returned, wide, ahead, back_rows, products):
    blocks, rows, lanes = received.shape
    width = blocks * lanes
    slots = rows // (2 * lats)
    wide[...] = received[...].astype(jnp.float32)
    pair = 2 * lanes
    source = lax.broadcasted_iota(jnp.int32, (pair, pair), 0)
    target = lax.broadcasted_iota(jnp.int32, (pair, pair), 1)
    advance = (source == target // F * F + (target + 1) % F).astype(jnp.bfloat16)
    for i in range(0, blocks, 2):
        both = jnp.concatenate([received[i], received[i + 1]], axis=1)
        moved = jnp.dot(both, advance, preferred_element_type=jnp.float32)
        ahead[i] = moved[:, :lanes]
        ahead[i + 1] = moved[:, lanes:]

    def span(lat, part):
        return pl.ds(2 * lat + part, slots, stride=2 * lats)

    def gather(rows_of, lat):
        parts = [
            jnp.concatenate([rows_of[i, span(lat, part), :] for i in range(blocks)], axis=1)
            for part in range(2)
        ]
        return jnp.concatenate(parts, axis=0).astype(jnp.bfloat16)

    for lat in range(lats):
        field, partner = (
            jnp.dot(synthesis[...], gather(rows_of, lat), preferred_element_type=jnp.float32)
            for rows_of in (wide, ahead)
        )
        products[lat] = (field * partner).astype(jnp.bfloat16)
    for lat in range(lats):
        back = jnp.dot(analysis[...], products[lat], preferred_element_type=jnp.float32)
        for part in range(2):
            for i in range(blocks):
                back_rows[i, span(lat, part), :] = back[
                    part * slots : (part + 1) * slots, i * lanes : (i + 1) * lanes
                ]
    for i in range(blocks):
        returned[:, i * lanes : (i + 1) * lanes] = back_rows[i].astype(jnp.bfloat16)


def own_kernel(own, own_matrix, total):
    total[...] = jnp.dot(own[...], own_matrix[...], preferred_element_type=jnp.float32)


def couple_kernel(begun, other, other_matrix, weight, sent):
    total = begun[...] + jnp.dot(other[...], other_matrix[...], preferred_element_type=jnp.float32)
    total *= weight[...]
    blocks, rows, lanes = sent.shape
    for i in range(blocks):
        sent[i] = total[:, i * lanes : (i + 1) * lanes].astype(jnp.bfloat16)


def call(kernel, out_shape, flops, limit, *operands, scratch=()):
    moved = sum(x.size * x.dtype.itemsize for x in operands) + out_shape.size * 2
    return pl.pallas_call(
        kernel,
        out_shape=out_shape,
        in_specs=[pl.BlockSpec(memory_space=pltpu.VMEM)] * len(operands),
        out_specs=pl.BlockSpec(memory_space=pltpu.VMEM),
        scratch_shapes=scratch,
        compiler_params=pltpu.CompilerParams(vmem_limit_bytes=limit << 20),
        cost_estimate=pl.CostEstimate(flops=flops, bytes_accessed=moved, transcendentals=0),
    )(*operands)


def local(spectral, legendre, pattern, assignment, quad_weight, coupling):
    degrees = spectral.shape[1]
    channels = spectral.shape[3]
    lat_count = legendre.shape[1]
    wave_total = assignment.shape[0]
    y_count = SIZES["y"]
    peers = y_count * wave_total
    lats = lat_count // peers
    rows = wave_total * lats * 2
    own_levels = channels // F
    slot = lax.axis_index("z") * SIZES["x"] + lax.axis_index("x")
    core = lax.axis_index("core")

    own_wave = lax.dynamic_index_in_dim(assignment, slot, 0, keepdims=False)
    own_mask = lax.dynamic_index_in_dim(pattern, own_wave, 0, keepdims=False).astype(jnp.bfloat16)
    lat_tiles, deg_tiles = own_mask.shape
    wide_mask = jnp.broadcast_to(
        own_mask[:, None, :, None], (lat_tiles, TILE, deg_tiles, TILE)
    ).reshape(lat_count, degrees)
    pruned = legendre[0] * wide_mask

    at_lats = forward(spectral[0], legendre[0], pattern, assignment)
    at_lats = at_lats.reshape(peers, lats, 2, channels)
    received = exchange(at_lats)
    received = received.reshape(y_count, rows, channels)

    arrival = assignment.reshape(SIZES["z"], SIZES["x"])
    arrival = jnp.roll(arrival, (-middle("z"), -middle("x")), (0, 1)).T.reshape(wave_total)
    lon_count = 3 * wave_total
    synthesis, analysis = wave_tables(arrival, lon_count)
    cores = SIZES["core"]
    split = coupling.reshape(y_count, cores, own_levels, y_count, cores, own_levels)
    split = jnp.roll(split, (-middle("y"), -middle("y")), (0, 3))
    mine = lax.dynamic_index_in_dim(split, core, 1, keepdims=False)
    wide = y_count * channels
    spread = (
        jnp.arange(wide, dtype=jnp.int32)[:, None] // F
        == jnp.arange(wide // F, dtype=jnp.int32)[None, :]
    ).astype(jnp.bfloat16)
    same_field = (
        jnp.arange(wide, dtype=jnp.int32)[:, None] % F
        == jnp.arange(wide, dtype=jnp.int32)[None, :] % F
    )

    def matrix(source):
        small = lax.dynamic_index_in_dim(mine, source, 3, keepdims=False)
        small = small.reshape(wide // F, wide // F)
        tall = jnp.einsum("pb,ab->pa", spread, small).astype(jnp.bfloat16)
        full = jnp.einsum("pa,qa->pq", tall, spread).astype(jnp.bfloat16)
        return jnp.where(same_field, full, jnp.zeros((), jnp.bfloat16))

    group = own_position()
    weight = lax.dynamic_slice_in_dim(quad_weight, group * lats, lats)
    weight = jnp.broadcast_to(weight[None, :, None], (wave_total, lats, 2)).reshape(rows, 1)
    own_matrix, other_matrix = matrix(core), matrix(1 - core)
    received, synthesis, analysis, own_matrix, other_matrix, weight, pruned = (
        lax.optimization_barrier(
            (received, synthesis, analysis, own_matrix, other_matrix, weight, pruned)
        )
    )

    wide = y_count * channels
    flops = 4 * lon_count * rows * wide
    returned = call(
        functools.partial(grid_kernel, lats),
        jax.ShapeDtypeStruct((rows, wide), jnp.bfloat16),
        flops,
        16,
        received,
        synthesis,
        analysis,
        scratch=[pltpu.VMEM((y_count, rows, channels), jnp.float32)] * 3
        + [pltpu.VMEM((lats, lon_count, wide), jnp.bfloat16)],
    )
    swapped = lax.ppermute(returned, "core", [(0, 1), (1, 0)])

    begun = call(
        own_kernel,
        jax.ShapeDtypeStruct((rows, wide), jnp.float32),
        2 * rows * wide * wide,
        16,
        returned,
        own_matrix,
    )
    sent = call(
        couple_kernel,
        jax.ShapeDtypeStruct((y_count, rows, channels), jnp.bfloat16),
        2 * rows * wide * wide,
        16,
        begun,
        swapped,
        other_matrix,
        weight,
    )
    sent = sent.reshape(peers, lats, 2, channels)
    weighted = exchange(sent)
    weighted = weighted.reshape(lat_count, 2, channels)
    tendency = jnp.einsum("ln,lch->nch", pruned, weighted, preferred_element_type=jnp.float32)
    return tendency.astype(jnp.bfloat16)[None]


def solution(mesh):
    grid = Mesh(mesh.devices.reshape(tuple(SIZES.values())), tuple(SIZES))
    wave, lev = ("z", "x"), ("y", "core")
    placed = (P(wave, None, None, lev), P(wave, None, None), P(), P(), P(), P())
    return jax.shard_map(
        local,
        mesh=grid,
        in_specs=placed,
        out_specs=P(wave, None, None, lev),
        check_vma=False,
    )
```

```python
import functools
import math

import jax
import jax.numpy as jnp
from jax import lax
from jax.experimental import pallas as pl
from jax.experimental.pallas import tpu as pltpu
from jax.sharding import Mesh
from jax.sharding import PartitionSpec as P

F = 8
TILE = 128
LAT_CHUNKS = 2
LAT_PARTS = 2
PEERS = ("y", "x", "z")
SIZES = {"z": 16, "x": 4, "y": 4, "core": 2}


def middle(axis):
    return SIZES[axis] // 2


def peer_groups():
    order = [
        [(place + middle(axis)) % SIZES[axis] for place in range(SIZES[axis])] for axis in PEERS
    ]
    return [
        [
            ((z * SIZES["x"] + x) * SIZES["y"] + y) * SIZES["core"] + core
            for y in order[0]
            for x in order[1]
            for z in order[2]
        ]
        for core in range(SIZES["core"])
    ]


def own_position():
    position = 0
    for axis in PEERS:
        place = lax.rem(lax.axis_index(axis) + middle(axis), SIZES[axis])
        position = position * SIZES[axis] + place
    return position


def exchange(values):
    return lax.all_to_all(
        values,
        tuple(SIZES),
        split_axis=0,
        concat_axis=0,
        axis_index_groups=peer_groups(),
        tiled=True,
    )


def wave_tables(waves, lon_count):
    wave_total = waves.shape[0]
    longitudes = jnp.arange(lon_count, dtype=jnp.int32)
    phases = longitudes[:, None] * waves[None, :] % lon_count
    angles = phases.astype(jnp.float32) * (2.0 * math.pi / lon_count)
    basis = jnp.concatenate([jnp.cos(angles), -jnp.sin(angles)], axis=1)
    synthesis = (basis / math.sqrt(wave_total)).astype(jnp.bfloat16)
    analysis = (basis.T / math.sqrt(lon_count)).astype(jnp.bfloat16)
    return synthesis, analysis


def forward_kernel(
    spectral, legendre, pattern, assignment, at_lats,
    raw, matrix, blocks, waves, paired, coeffs, wide, merged, in_sem, lat_sem, out_sem,
):
    lat_tiles, deg_tiles, _ = pattern.shape
    lat_count, degrees = legendre.shape
    lanes = raw.shape[1]
    chunk = lat_count // LAT_CHUNKS
    copies = [
        pltpu.make_async_copy(source, target, in_sem.at[i])
        for i, (source, target) in enumerate(
            ((spectral, raw), (assignment, waves), (pattern, blocks))
        )
    ]
    for copy in copies:
        copy.start()

    def lat_copy(i):
        span = pl.ds(i * chunk, chunk)
        return pltpu.make_async_copy(legendre.at[span], matrix.at[span], lat_sem.at[i])

    def out_copy(i):
        span = pl.ds(2 * i * chunk, 2 * chunk)
        return pltpu.make_async_copy(merged.at[span], at_lats.at[span], out_sem.at[i])

    for i in range(LAT_CHUNKS):
        lat_copy(i).start()
    copies[0].wait()
    paired[...] = raw[...].astype(jnp.float32)
    for part in range(2):
        coeffs[:, part * lanes : (part + 1) * lanes] = paired[
            pl.ds(part, degrees, stride=2), :
        ].astype(jnp.bfloat16)
    copies[1].wait()
    copies[2].wait()
    slot = lax.axis_index("z") * SIZES["x"] + lax.axis_index("x")
    wave = waves[slot]
    picked = lax.broadcasted_iota(jnp.int32, blocks.shape, 2) == wave
    mask = jnp.sum(jnp.where(picked, blocks[...], 0), axis=2, keepdims=True)
    for i in range(LAT_CHUNKS):
        lat_copy(i).wait()
        for t in range(i * lat_tiles // LAT_CHUNKS, (i + 1) * lat_tiles // LAT_CHUNKS):
            keep = jnp.concatenate(
                [
                    jnp.broadcast_to(mask[t, k : k + 1, :], (TILE, TILE)).astype(jnp.bfloat16)
                    for k in range(deg_tiles)
                ],
                axis=1,
            )
            tile = slice(TILE * t, TILE * (t + 1))
            matrix[tile, :] = matrix[tile, :] * keep
        depth = chunk // LAT_PARTS
        founds = [
            jnp.dot(
                matrix[pl.ds(chunk * i + depth * j, depth), :],
                coeffs[...],
                preferred_element_type=jnp.float32,
            )
            for j in range(LAT_PARTS)
        ]
        for j, found in enumerate(founds):
            for part in range(2):
                wide[pl.ds(2 * depth * j + part, depth, stride=2), :] = found[
                    :, part * lanes : (part + 1) * lanes
                ]
        merged[2 * chunk * i : 2 * chunk * (i + 1), :] = wide[...].astype(jnp.bfloat16)
        out_copy(i).start()
    for i in range(LAT_CHUNKS):
        out_copy(i).wait()


def forward(spectral, legendre, pattern, assignment):
    degrees, _, channels = spectral.shape
    lat_count = legendre.shape[0]
    pattern = jnp.transpose(pattern, (1, 2, 0))
    chunk = lat_count // LAT_CHUNKS
    return pl.pallas_call(
        forward_kernel,
        out_shape=jax.ShapeDtypeStruct((2 * lat_count, channels), jnp.bfloat16),
        in_specs=[pl.BlockSpec(memory_space=pltpu.HBM)] * 4,
        out_specs=pl.BlockSpec(memory_space=pltpu.HBM),
        scratch_shapes=[
            pltpu.VMEM((2 * degrees, channels), jnp.bfloat16),
            pltpu.VMEM((lat_count, degrees), jnp.bfloat16),
            pltpu.VMEM(pattern.shape, jnp.int32),
            pltpu.SMEM(assignment.shape, jnp.int32),
            pltpu.VMEM((2 * degrees, channels), jnp.float32),
            pltpu.VMEM((degrees, 2 * channels), jnp.bfloat16),
            pltpu.VMEM((2 * chunk, channels), jnp.float32),
            pltpu.VMEM((2 * lat_count, channels), jnp.bfloat16),
            pltpu.SemaphoreType.DMA((3,)),
            pltpu.SemaphoreType.DMA((LAT_CHUNKS,)),
            pltpu.SemaphoreType.DMA((LAT_CHUNKS,)),
        ],
    )(spectral.reshape(2 * degrees, channels), legendre, pattern, assignment)


def grid_kernel(lats, received, synthesis, analysis, returned, wide, ahead, back_rows, products):
    blocks, rows, lanes = received.shape
    width = blocks * lanes
    slots = rows // (2 * lats)
    wide[...] = received[...].astype(jnp.float32)
    pair = 2 * lanes
    source = lax.broadcasted_iota(jnp.int32, (pair, pair), 0)
    target = lax.broadcasted_iota(jnp.int32, (pair, pair), 1)
    advance = (source == target // F * F + (target + 1) % F).astype(jnp.bfloat16)
    for i in range(0, blocks, 2):
        both = jnp.concatenate([received[i], received[i + 1]], axis=1)
        moved = jnp.dot(both, advance, preferred_element_type=jnp.float32)
        ahead[i] = moved[:, :lanes]
        ahead[i + 1] = moved[:, lanes:]

    def span(lat, part):
        return pl.ds(2 * lat + part, slots, stride=2 * lats)

    def gather(rows_of, lat):
        parts = [
            jnp.concatenate([rows_of[i, span(lat, part), :] for i in range(blocks)], axis=1)
            for part in range(2)
        ]
        return jnp.concatenate(parts, axis=0).astype(jnp.bfloat16)

    for lat in range(lats):
        field, partner = (
            jnp.dot(synthesis[...], gather(rows_of, lat), preferred_element_type=jnp.float32)
            for rows_of in (wide, ahead)
        )
        products[lat] = (field * partner).astype(jnp.bfloat16)
    for lat in range(lats):
        back = jnp.dot(analysis[...], products[lat], preferred_element_type=jnp.float32)
        for part in range(2):
            for i in range(blocks):
                back_rows[i, span(lat, part), :] = back[
                    part * slots : (part + 1) * slots, i * lanes : (i + 1) * lanes
                ]
    for i in range(blocks):
        returned[:, i * lanes : (i + 1) * lanes] = back_rows[i].astype(jnp.bfloat16)


def own_kernel(own, own_matrix, total):
    total[...] = jnp.dot(own[...], own_matrix[...], preferred_element_type=jnp.float32)


def couple_kernel(begun, other, other_matrix, weight, sent):
    total = begun[...] + jnp.dot(other[...], other_matrix[...], preferred_element_type=jnp.float32)
    total *= weight[...]
    blocks, rows, lanes = sent.shape
    for i in range(blocks):
        sent[i] = total[:, i * lanes : (i + 1) * lanes].astype(jnp.bfloat16)


def backward_kernel(weighted, pruned_t, result, paired, coeffs, wide, merged, out_sem):
    degrees, lat_count = pruned_t.shape
    lanes = weighted.shape[1]
    paired[...] = weighted[...].astype(jnp.float32)
    for part in range(2):
        coeffs[:, part * lanes : (part + 1) * lanes] = paired[
            pl.ds(part, lat_count, stride=2), :
        ].astype(jnp.bfloat16)
    depth = degrees // 2
    founds = [
        jnp.dot(
            pruned_t[depth * j : depth * (j + 1), :],
            coeffs[...],
            preferred_element_type=jnp.float32,
        )
        for j in range(2)
    ]
    copies = []
    for j, found in enumerate(founds):
        for part in range(2):
            wide[pl.ds(2 * depth * j + part, depth, stride=2), :] = found[
                :, part * lanes : (part + 1) * lanes
            ]
        span = pl.ds(2 * depth * j, 2 * depth)
        merged[span, :] = wide[span, :].astype(jnp.bfloat16)
        copy = pltpu.make_async_copy(merged.at[span], result.at[span], out_sem.at[j])
        copy.start()
        copies.append(copy)
    for copy in copies:
        copy.wait()


def backward(weighted, pruned_t):
    degrees, lat_count = pruned_t.shape
    channels = weighted.shape[1]
    return pl.pallas_call(
        backward_kernel,
        out_shape=jax.ShapeDtypeStruct((2 * degrees, channels), jnp.bfloat16),
        in_specs=[pl.BlockSpec(memory_space=pltpu.VMEM)] * 2,
        out_specs=pl.BlockSpec(memory_space=pltpu.HBM),
        scratch_shapes=[
            pltpu.VMEM((2 * lat_count, channels), jnp.float32),
            pltpu.VMEM((lat_count, 2 * channels), jnp.bfloat16),
            pltpu.VMEM((2 * degrees, channels), jnp.float32),
            pltpu.VMEM((2 * degrees, channels), jnp.bfloat16),
            pltpu.SemaphoreType.DMA((2,)),
        ],
        compiler_params=pltpu.CompilerParams(vmem_limit_bytes=16 << 20),
    )(weighted, pruned_t)


def call(kernel, out_shape, flops, limit, *operands, scratch=()):
    moved = sum(x.size * x.dtype.itemsize for x in operands) + out_shape.size * 2
    return pl.pallas_call(
        kernel,
        out_shape=out_shape,
        in_specs=[pl.BlockSpec(memory_space=pltpu.VMEM)] * len(operands),
        out_specs=pl.BlockSpec(memory_space=pltpu.VMEM),
        scratch_shapes=scratch,
        compiler_params=pltpu.CompilerParams(vmem_limit_bytes=limit << 20),
        cost_estimate=pl.CostEstimate(flops=flops, bytes_accessed=moved, transcendentals=0),
    )(*operands)


def local(spectral, legendre, pattern, assignment, quad_weight, coupling):
    degrees = spectral.shape[1]
    channels = spectral.shape[3]
    lat_count = legendre.shape[1]
    wave_total = assignment.shape[0]
    y_count = SIZES["y"]
    peers = y_count * wave_total
    lats = lat_count // peers
    rows = wave_total * lats * 2
    own_levels = channels // F
    slot = lax.axis_index("z") * SIZES["x"] + lax.axis_index("x")
    core = lax.axis_index("core")

    own_wave = lax.dynamic_index_in_dim(assignment, slot, 0, keepdims=False)
    own_mask = lax.dynamic_index_in_dim(pattern, own_wave, 0, keepdims=False).astype(jnp.bfloat16)
    at_lats = forward(spectral[0], legendre[0], pattern, assignment)
    at_lats = at_lats.reshape(peers, lats, 2, channels)
    received = exchange(at_lats)
    received = received.reshape(y_count, rows, channels)

    arrival = assignment.reshape(SIZES["z"], SIZES["x"])
    arrival = jnp.roll(arrival, (-middle("z"), -middle("x")), (0, 1)).T.reshape(wave_total)
    lon_count = 3 * wave_total
    synthesis, analysis = wave_tables(arrival, lon_count)
    cores = SIZES["core"]
    split = coupling.reshape(y_count, cores, own_levels, y_count, cores, own_levels)
    split = jnp.roll(split, (-middle("y"), -middle("y")), (0, 3))
    mine = lax.dynamic_index_in_dim(split, core, 1, keepdims=False)
    wide = y_count * channels
    spread = (
        jnp.arange(wide, dtype=jnp.int32)[:, None] // F
        == jnp.arange(wide // F, dtype=jnp.int32)[None, :]
    ).astype(jnp.bfloat16)
    same_field = (
        jnp.arange(wide, dtype=jnp.int32)[:, None] % F
        == jnp.arange(wide, dtype=jnp.int32)[None, :] % F
    )

    def matrix(source):
        small = lax.dynamic_index_in_dim(mine, source, 3, keepdims=False)
        small = small.reshape(wide // F, wide // F)
        tall = jnp.einsum("pb,ab->pa", spread, small).astype(jnp.bfloat16)
        full = jnp.einsum("pa,qa->pq", tall, spread).astype(jnp.bfloat16)
        return jnp.where(same_field, full, jnp.zeros((), jnp.bfloat16))

    group = own_position()
    weight = lax.dynamic_slice_in_dim(quad_weight, group * lats, lats)
    weight = jnp.broadcast_to(weight[None, :, None], (wave_total, lats, 2)).reshape(rows, 1)
    own_matrix, other_matrix = matrix(core), matrix(1 - core)
    received, synthesis, analysis, own_matrix, other_matrix, weight, own_mask = (
        lax.optimization_barrier(
            (received, synthesis, analysis, own_matrix, other_matrix, weight, own_mask)
        )
    )

    wide = y_count * channels
    flops = 4 * lon_count * rows * wide
    returned = call(
        functools.partial(grid_kernel, lats),
        jax.ShapeDtypeStruct((rows, wide), jnp.bfloat16),
        flops,
        16,
        received,
        synthesis,
        analysis,
        scratch=[pltpu.VMEM((y_count, rows, channels), jnp.float32)] * 3
        + [pltpu.VMEM((lats, lon_count, wide), jnp.bfloat16)],
    )
    swapped = lax.ppermute(returned, "core", [(0, 1), (1, 0)])

    begun = call(
        own_kernel,
        jax.ShapeDtypeStruct((rows, wide), jnp.float32),
        2 * rows * wide * wide,
        16,
        returned,
        own_matrix,
    )
    sent = call(
        couple_kernel,
        jax.ShapeDtypeStruct((y_count, rows, channels), jnp.bfloat16),
        2 * rows * wide * wide,
        16,
        begun,
        swapped,
        other_matrix,
        weight,
    )
    sent, own_mask = lax.optimization_barrier((sent, own_mask))
    lat_tiles, deg_tiles = own_mask.shape
    wide_mask = jnp.broadcast_to(
        own_mask[:, None, :, None], (lat_tiles, TILE, deg_tiles, TILE)
    ).reshape(lat_count, degrees)
    pruned_t = (legendre[0] * wide_mask).T
    sent = sent.reshape(peers, lats, 2, channels)
    weighted = exchange(sent)
    tendency = backward(weighted.reshape(2 * lat_count, channels), pruned_t)
    return tendency.reshape(1, degrees, 2, channels)


def solution(mesh):
    grid = Mesh(mesh.devices.reshape(tuple(SIZES.values())), tuple(SIZES))
    wave, lev = ("z", "x"), ("y", "core")
    placed = (P(wave, None, None, lev), P(wave, None, None), P(), P(), P(), P())
    return jax.shard_map(
        local,
        mesh=grid,
        in_specs=placed,
        out_specs=P(wave, None, None, lev),
        check_vma=False,
    )
```

```python
import functools
import math

import jax
import jax.numpy as jnp
from jax import lax
from jax.experimental import pallas as pl
from jax.experimental.pallas import tpu as pltpu
from jax.sharding import Mesh
from jax.sharding import PartitionSpec as P

F = 8
TILE = 128
LAT_CHUNKS = 2
LAT_PARTS = 2
PEERS = ("y", "x", "z")
SIZES = {"z": 16, "x": 4, "y": 4, "core": 2}


def middle(axis):
    return SIZES[axis] // 2


def peer_groups():
    order = [
        [(place + middle(axis)) % SIZES[axis] for place in range(SIZES[axis])] for axis in PEERS
    ]
    return [
        [
            ((z * SIZES["x"] + x) * SIZES["y"] + y) * SIZES["core"] + core
            for y in order[0]
            for x in order[1]
            for z in order[2]
        ]
        for core in range(SIZES["core"])
    ]


def own_position():
    position = 0
    for axis in PEERS:
        place = lax.rem(lax.axis_index(axis) + middle(axis), SIZES[axis])
        position = position * SIZES[axis] + place
    return position


def exchange(values):
    return lax.all_to_all(
        values,
        tuple(SIZES),
        split_axis=0,
        concat_axis=0,
        axis_index_groups=peer_groups(),
        tiled=True,
    )


def wave_tables(waves, lon_count):
    wave_total = waves.shape[0]
    longitudes = jnp.arange(lon_count, dtype=jnp.int32)
    phases = longitudes[:, None] * waves[None, :] % lon_count
    angles = phases.astype(jnp.float32) * (2.0 * math.pi / lon_count)
    basis = jnp.concatenate([jnp.cos(angles), -jnp.sin(angles)], axis=1)
    synthesis = (basis / math.sqrt(wave_total)).astype(jnp.bfloat16)
    analysis = (basis.T / math.sqrt(lon_count)).astype(jnp.bfloat16)
    return synthesis, analysis


def forward_kernel(
    spectral, legendre, pattern, assignment, at_lats,
    raw, matrix, blocks, waves, paired, coeffs, wide, merged, in_sem, lat_sem, out_sem,
):
    lat_tiles, deg_tiles, _ = pattern.shape
    lat_count, degrees = legendre.shape
    lanes = raw.shape[1]
    chunk = lat_count // LAT_CHUNKS
    copies = [
        pltpu.make_async_copy(source, target, in_sem.at[i])
        for i, (source, target) in enumerate(
            ((spectral, raw), (assignment, waves), (pattern, blocks))
        )
    ]
    for copy in copies:
        copy.start()

    def lat_copy(i):
        span = pl.ds(i * chunk, chunk)
        return pltpu.make_async_copy(legendre.at[span], matrix.at[span], lat_sem.at[i])

    def out_copy(i):
        span = pl.ds(2 * i * chunk, 2 * chunk)
        return pltpu.make_async_copy(merged.at[span], at_lats.at[span], out_sem.at[i])

    for i in range(LAT_CHUNKS):
        lat_copy(i).start()
    copies[0].wait()
    paired[...] = raw[...].astype(jnp.float32)
    for part in range(2):
        coeffs[:, part * lanes : (part + 1) * lanes] = paired[
            pl.ds(part, degrees, stride=2), :
        ].astype(jnp.bfloat16)
    copies[1].wait()
    copies[2].wait()
    slot = lax.axis_index("z") * SIZES["x"] + lax.axis_index("x")
    wave = waves[slot]
    picked = lax.broadcasted_iota(jnp.int32, blocks.shape, 2) == wave
    mask = jnp.sum(jnp.where(picked, blocks[...], 0), axis=2, keepdims=True)
    for i in range(LAT_CHUNKS):
        lat_copy(i).wait()
        for t in range(i * lat_tiles // LAT_CHUNKS, (i + 1) * lat_tiles // LAT_CHUNKS):
            keep = jnp.concatenate(
                [
                    jnp.broadcast_to(mask[t, k : k + 1, :], (TILE, TILE)).astype(jnp.bfloat16)
                    for k in range(deg_tiles)
                ],
                axis=1,
            )
            tile = slice(TILE * t, TILE * (t + 1))
            matrix[tile, :] = matrix[tile, :] * keep
        depth = chunk // LAT_PARTS
        founds = [
            jnp.dot(
                matrix[pl.ds(chunk * i + depth * j, depth), :],
                coeffs[...],
                preferred_element_type=jnp.float32,
            )
            for j in range(LAT_PARTS)
        ]
        for j, found in enumerate(founds):
            for part in range(2):
                wide[pl.ds(2 * depth * j + part, depth, stride=2), :] = found[
                    :, part * lanes : (part + 1) * lanes
                ]
        merged[2 * chunk * i : 2 * chunk * (i + 1), :] = wide[...].astype(jnp.bfloat16)
        out_copy(i).start()
    for i in range(LAT_CHUNKS):
        out_copy(i).wait()


def forward(spectral, legendre, pattern, assignment):
    degrees, _, channels = spectral.shape
    lat_count = legendre.shape[0]
    pattern = jnp.transpose(pattern, (1, 2, 0))
    chunk = lat_count // LAT_CHUNKS
    return pl.pallas_call(
        forward_kernel,
        out_shape=jax.ShapeDtypeStruct((2 * lat_count, channels), jnp.bfloat16),
        in_specs=[pl.BlockSpec(memory_space=pltpu.HBM)] * 4,
        out_specs=pl.BlockSpec(memory_space=pltpu.HBM),
        scratch_shapes=[
            pltpu.VMEM((2 * degrees, channels), jnp.bfloat16),
            pltpu.VMEM((lat_count, degrees), jnp.bfloat16),
            pltpu.VMEM(pattern.shape, jnp.int32),
            pltpu.SMEM(assignment.shape, jnp.int32),
            pltpu.VMEM((2 * degrees, channels), jnp.float32),
            pltpu.VMEM((degrees, 2 * channels), jnp.bfloat16),
            pltpu.VMEM((2 * chunk, channels), jnp.float32),
            pltpu.VMEM((2 * lat_count, channels), jnp.bfloat16),
            pltpu.SemaphoreType.DMA((3,)),
            pltpu.SemaphoreType.DMA((LAT_CHUNKS,)),
            pltpu.SemaphoreType.DMA((LAT_CHUNKS,)),
        ],
    )(spectral.reshape(2 * degrees, channels), legendre, pattern, assignment)


def grid_kernel(
    lats, received, synthesis, analysis, weight, returned, wide, ahead, back_rows, products
):
    blocks, rows, lanes = received.shape
    width = blocks * lanes
    slots = rows // (2 * lats)
    wide[...] = received[...].astype(jnp.float32)
    pair = 2 * lanes
    source = lax.broadcasted_iota(jnp.int32, (pair, pair), 0)
    target = lax.broadcasted_iota(jnp.int32, (pair, pair), 1)
    advance = (source == target // F * F + (target + 1) % F).astype(jnp.bfloat16)
    for i in range(0, blocks, 2):
        both = jnp.concatenate([received[i], received[i + 1]], axis=1)
        moved = jnp.dot(both, advance, preferred_element_type=jnp.float32)
        ahead[i] = moved[:, :lanes]
        ahead[i + 1] = moved[:, lanes:]

    def span(lat, part):
        return pl.ds(2 * lat + part, slots, stride=2 * lats)

    def gather(rows_of, lat):
        parts = [
            jnp.concatenate([rows_of[i, span(lat, part), :] for i in range(blocks)], axis=1)
            for part in range(2)
        ]
        return jnp.concatenate(parts, axis=0).astype(jnp.bfloat16)

    for lat in range(lats):
        field, partner = (
            jnp.dot(synthesis[...], gather(rows_of, lat), preferred_element_type=jnp.float32)
            for rows_of in (wide, ahead)
        )
        products[lat] = (field * partner).astype(jnp.bfloat16)
    for lat in range(lats):
        back = jnp.dot(analysis[...], products[lat], preferred_element_type=jnp.float32)
        back = back * weight[lat : lat + 1, :]
        for part in range(2):
            for i in range(blocks):
                back_rows[i, span(lat, part), :] = back[
                    part * slots : (part + 1) * slots, i * lanes : (i + 1) * lanes
                ]
    for i in range(blocks):
        returned[:, i * lanes : (i + 1) * lanes] = back_rows[i].astype(jnp.bfloat16)


def level_matrix(small, width):
    levels = small.shape[0]
    channel = lax.broadcasted_iota(jnp.int32, (width, levels), 0) // F
    level = lax.broadcasted_iota(jnp.int32, (width, levels), 1)
    spread = (channel == level).astype(jnp.bfloat16)
    contract = (((1,), (1,)), ((), ()))
    tall = lax.dot_general(spread, small, contract, preferred_element_type=jnp.float32)
    tall = tall.astype(jnp.bfloat16)
    full = lax.dot_general(tall, spread, contract, preferred_element_type=jnp.float32)
    source = lax.broadcasted_iota(jnp.int32, (width, width), 0) % F
    target = lax.broadcasted_iota(jnp.int32, (width, width), 1) % F
    return jnp.where(source == target, full, 0.0).astype(jnp.bfloat16)


def own_kernel(own, own_small, other_small, total, other_matrix):
    width = own.shape[1]
    total[...] = jnp.dot(
        own[...], level_matrix(own_small[...], width), preferred_element_type=jnp.float32
    )
    other_matrix[...] = level_matrix(other_small[...], width)


def couple_kernel(begun, other, other_matrix, sent):
    total = begun[...] + jnp.dot(other[...], other_matrix[...], preferred_element_type=jnp.float32)
    blocks, rows, lanes = sent.shape
    for i in range(blocks):
        sent[i] = total[:, i * lanes : (i + 1) * lanes].astype(jnp.bfloat16)


def backward_kernel(weighted, pruned_t, result, paired, coeffs, wide, merged, out_sem):
    degrees, lat_count = pruned_t.shape
    lanes = weighted.shape[1]
    paired[...] = weighted[...].astype(jnp.float32)
    for part in range(2):
        coeffs[:, part * lanes : (part + 1) * lanes] = paired[
            pl.ds(part, lat_count, stride=2), :
        ].astype(jnp.bfloat16)
    depth = degrees // 2
    founds = [
        jnp.dot(
            pruned_t[depth * j : depth * (j + 1), :],
            coeffs[...],
            preferred_element_type=jnp.float32,
        )
        for j in range(2)
    ]
    copies = []
    for j, found in enumerate(founds):
        for part in range(2):
            wide[pl.ds(2 * depth * j + part, depth, stride=2), :] = found[
                :, part * lanes : (part + 1) * lanes
            ]
        span = pl.ds(2 * depth * j, 2 * depth)
        merged[span, :] = wide[span, :].astype(jnp.bfloat16)
        copy = pltpu.make_async_copy(merged.at[span], result.at[span], out_sem.at[j])
        copy.start()
        copies.append(copy)
    for copy in copies:
        copy.wait()


def backward(weighted, pruned_t):
    degrees, lat_count = pruned_t.shape
    channels = weighted.shape[1]
    return pl.pallas_call(
        backward_kernel,
        out_shape=jax.ShapeDtypeStruct((2 * degrees, channels), jnp.bfloat16),
        in_specs=[pl.BlockSpec(memory_space=pltpu.VMEM)] * 2,
        out_specs=pl.BlockSpec(memory_space=pltpu.HBM),
        scratch_shapes=[
            pltpu.VMEM((2 * lat_count, channels), jnp.float32),
            pltpu.VMEM((lat_count, 2 * channels), jnp.bfloat16),
            pltpu.VMEM((2 * degrees, channels), jnp.float32),
            pltpu.VMEM((2 * degrees, channels), jnp.bfloat16),
            pltpu.SemaphoreType.DMA((2,)),
        ],
        compiler_params=pltpu.CompilerParams(vmem_limit_bytes=16 << 20),
    )(weighted, pruned_t)


def call(kernel, out_shape, flops, limit, *operands, scratch=()):
    arrays = (*operands, *jax.tree.leaves(out_shape))
    moved = sum(x.size * x.dtype.itemsize for x in arrays)
    return pl.pallas_call(
        kernel,
        out_shape=out_shape,
        in_specs=[pl.BlockSpec(memory_space=pltpu.VMEM)] * len(operands),
        out_specs=jax.tree.map(lambda _: pl.BlockSpec(memory_space=pltpu.VMEM), out_shape),
        scratch_shapes=scratch,
        compiler_params=pltpu.CompilerParams(vmem_limit_bytes=limit << 20),
        cost_estimate=pl.CostEstimate(flops=flops, bytes_accessed=moved, transcendentals=0),
    )(*operands)


def local(spectral, legendre, pattern, assignment, quad_weight, coupling):
    degrees = spectral.shape[1]
    channels = spectral.shape[3]
    lat_count = legendre.shape[1]
    wave_total = assignment.shape[0]
    y_count = SIZES["y"]
    peers = y_count * wave_total
    lats = lat_count // peers
    rows = wave_total * lats * 2
    own_levels = channels // F
    slot = lax.axis_index("z") * SIZES["x"] + lax.axis_index("x")
    core = lax.axis_index("core")

    own_wave = lax.dynamic_index_in_dim(assignment, slot, 0, keepdims=False)
    own_mask = lax.dynamic_index_in_dim(pattern, own_wave, 0, keepdims=False).astype(jnp.bfloat16)
    lat_tiles, deg_tiles = own_mask.shape
    wide_mask = jnp.broadcast_to(
        own_mask[:, None, :, None], (lat_tiles, TILE, deg_tiles, TILE)
    ).reshape(lat_count, degrees)
    pruned = legendre[0] * wide_mask

    at_lats = forward(spectral[0], legendre[0], pattern, assignment)
    at_lats = at_lats.reshape(peers, lats, 2, channels)
    received = exchange(at_lats)
    received = received.reshape(y_count, rows, channels)

    arrival = assignment.reshape(SIZES["z"], SIZES["x"])
    arrival = jnp.roll(arrival, (-middle("z"), -middle("x")), (0, 1)).T.reshape(wave_total)
    lon_count = 3 * wave_total
    synthesis, analysis = wave_tables(arrival, lon_count)
    cores = SIZES["core"]
    split = coupling.reshape(y_count, cores, own_levels, y_count, cores, own_levels)
    split = jnp.roll(split, (-middle("y"), -middle("y")), (0, 3))
    mine = lax.dynamic_index_in_dim(split, core, 1, keepdims=False)
    wide = y_count * channels

    def matrix(source):
        small = lax.dynamic_index_in_dim(mine, source, 3, keepdims=False)
        return small.reshape(wide // F, wide // F)

    group = own_position()
    weight = lax.dynamic_slice_in_dim(quad_weight, group * lats, lats)
    weight = jnp.broadcast_to(weight[:, None], (lats, wide))
    own_small, other_small = matrix(core), matrix(1 - core)
    received, synthesis, analysis, own_small, other_small, weight, pruned_t = (
        lax.optimization_barrier(
            (received, synthesis, analysis, own_small, other_small, weight, pruned.T)
        )
    )

    wide = y_count * channels
    flops = 4 * lon_count * rows * wide
    returned = call(
        functools.partial(grid_kernel, lats),
        jax.ShapeDtypeStruct((rows, wide), jnp.bfloat16),
        flops,
        16,
        received,
        synthesis,
        analysis,
        weight,
        scratch=[pltpu.VMEM((y_count, rows, channels), jnp.float32)] * 3
        + [pltpu.VMEM((lats, lon_count, wide), jnp.bfloat16)],
    )
    swapped = lax.ppermute(returned, "core", [(0, 1), (1, 0)])

    begun, other_matrix = call(
        own_kernel,
        (
            jax.ShapeDtypeStruct((rows, wide), jnp.float32),
            jax.ShapeDtypeStruct((wide, wide), jnp.bfloat16),
        ),
        2 * rows * wide * wide,
        16,
        returned,
        own_small,
        other_small,
    )
    sent = call(
        couple_kernel,
        jax.ShapeDtypeStruct((y_count, rows, channels), jnp.bfloat16),
        2 * rows * wide * wide,
        16,
        begun,
        swapped,
        other_matrix,
    )
    sent = sent.reshape(peers, lats, 2, channels)
    weighted = exchange(sent)
    tendency = backward(weighted.reshape(2 * lat_count, channels), pruned_t)
    return tendency.reshape(1, degrees, 2, channels)


def solution(mesh):
    grid = Mesh(mesh.devices.reshape(tuple(SIZES.values())), tuple(SIZES))
    wave, lev = ("z", "x"), ("y", "core")
    placed = (P(wave, None, None, lev), P(wave, None, None), P(), P(), P(), P())
    return jax.shard_map(
        local,
        mesh=grid,
        in_specs=placed,
        out_specs=P(wave, None, None, lev),
        check_vma=False,
    )
```

```python
import functools
import math

import jax
import jax.numpy as jnp
from jax import lax
from jax.experimental import pallas as pl
from jax.experimental.pallas import tpu as pltpu
from jax.sharding import Mesh
from jax.sharding import PartitionSpec as P

F = 8
TILE = 128
LAT_CHUNKS = 2
LAT_PARTS = 2
PEERS = ("y", "x", "z")
SIZES = {"z": 16, "x": 4, "y": 4, "core": 2}


def middle(axis):
    return SIZES[axis] // 2


def peer_groups():
    order = [
        [(place + middle(axis)) % SIZES[axis] for place in range(SIZES[axis])] for axis in PEERS
    ]
    return [
        [
            ((z * SIZES["x"] + x) * SIZES["y"] + y) * SIZES["core"] + core
            for y in order[0]
            for x in order[1]
            for z in order[2]
        ]
        for core in range(SIZES["core"])
    ]


def own_position():
    position = 0
    for axis in PEERS:
        place = lax.rem(lax.axis_index(axis) + middle(axis), SIZES[axis])
        position = position * SIZES[axis] + place
    return position


def exchange(values):
    return lax.all_to_all(
        values,
        tuple(SIZES),
        split_axis=0,
        concat_axis=0,
        axis_index_groups=peer_groups(),
        tiled=True,
    )


def wave_tables(waves, lon_count):
    wave_total = waves.shape[0]
    longitudes = jnp.arange(lon_count, dtype=jnp.int32)
    phases = longitudes[:, None] * waves[None, :] % lon_count
    angles = phases.astype(jnp.float32) * (2.0 * math.pi / lon_count)
    basis = jnp.concatenate([jnp.cos(angles), -jnp.sin(angles)], axis=1)
    synthesis = (basis / math.sqrt(wave_total)).astype(jnp.bfloat16)
    analysis = (basis.T / math.sqrt(lon_count)).astype(jnp.bfloat16)
    return synthesis, analysis


def forward_kernel(
    spectral, legendre, pattern, assignment, at_lats,
    raw, matrix, blocks, waves, paired, coeffs, wide, merged, in_sem, lat_sem, out_sem,
):
    lat_tiles, deg_tiles, _ = pattern.shape
    lat_count, degrees = legendre.shape
    lanes = raw.shape[1]
    chunk = lat_count // LAT_CHUNKS
    copies = [
        pltpu.make_async_copy(source, target, in_sem.at[i])
        for i, (source, target) in enumerate(
            ((spectral, raw), (assignment, waves), (pattern, blocks))
        )
    ]
    for copy in copies:
        copy.start()

    def lat_copy(i):
        span = pl.ds(i * chunk, chunk)
        return pltpu.make_async_copy(legendre.at[span], matrix.at[span], lat_sem.at[i])

    depth = chunk // LAT_PARTS

    def out_copy(i):
        span = pl.ds(2 * i * depth, 2 * depth)
        return pltpu.make_async_copy(merged.at[span], at_lats.at[span], out_sem.at[i])

    for i in range(LAT_CHUNKS):
        lat_copy(i).start()
    copies[0].wait()
    paired[...] = raw[...].astype(jnp.float32)
    for part in range(2):
        coeffs[:, part * lanes : (part + 1) * lanes] = paired[
            pl.ds(part, degrees, stride=2), :
        ].astype(jnp.bfloat16)
    copies[1].wait()
    copies[2].wait()
    slot = lax.axis_index("z") * SIZES["x"] + lax.axis_index("x")
    wave = waves[slot]
    picked = lax.broadcasted_iota(jnp.int32, blocks.shape, 2) == wave
    mask = jnp.sum(jnp.where(picked, blocks[...], 0), axis=2, keepdims=True)
    for i in range(LAT_CHUNKS):
        lat_copy(i).wait()
        for t in range(i * lat_tiles // LAT_CHUNKS, (i + 1) * lat_tiles // LAT_CHUNKS):
            keep = jnp.concatenate(
                [
                    jnp.broadcast_to(mask[t, k : k + 1, :], (TILE, TILE)).astype(jnp.bfloat16)
                    for k in range(deg_tiles)
                ],
                axis=1,
            )
            tile = slice(TILE * t, TILE * (t + 1))
            matrix[tile, :] = matrix[tile, :] * keep
        founds = [
            jnp.dot(
                matrix[pl.ds(chunk * i + depth * j, depth), :],
                coeffs[...],
                preferred_element_type=jnp.float32,
            )
            for j in range(LAT_PARTS)
        ]
        for j, found in enumerate(founds):
            for part in range(2):
                wide[pl.ds(2 * depth * j + part, depth, stride=2), :] = found[
                    :, part * lanes : (part + 1) * lanes
                ]
            first = 2 * (chunk * i + depth * j)
            merged[first : first + 2 * depth, :] = wide[
                2 * depth * j : 2 * depth * (j + 1), :
            ].astype(jnp.bfloat16)
            out_copy(i * LAT_PARTS + j).start()
    for i in range(LAT_CHUNKS * LAT_PARTS):
        out_copy(i).wait()


def forward(spectral, legendre, pattern, assignment):
    degrees, _, channels = spectral.shape
    lat_count = legendre.shape[0]
    pattern = jnp.transpose(pattern, (1, 2, 0))
    chunk = lat_count // LAT_CHUNKS
    return pl.pallas_call(
        forward_kernel,
        out_shape=jax.ShapeDtypeStruct((2 * lat_count, channels), jnp.bfloat16),
        in_specs=[pl.BlockSpec(memory_space=pltpu.HBM)] * 4,
        out_specs=pl.BlockSpec(memory_space=pltpu.HBM),
        scratch_shapes=[
            pltpu.VMEM((2 * degrees, channels), jnp.bfloat16),
            pltpu.VMEM((lat_count, degrees), jnp.bfloat16),
            pltpu.VMEM(pattern.shape, jnp.int32),
            pltpu.SMEM(assignment.shape, jnp.int32),
            pltpu.VMEM((2 * degrees, channels), jnp.float32),
            pltpu.VMEM((degrees, 2 * channels), jnp.bfloat16),
            pltpu.VMEM((2 * chunk, channels), jnp.float32),
            pltpu.VMEM((2 * lat_count, channels), jnp.bfloat16),
            pltpu.SemaphoreType.DMA((3,)),
            pltpu.SemaphoreType.DMA((LAT_CHUNKS,)),
            pltpu.SemaphoreType.DMA((LAT_CHUNKS * LAT_PARTS,)),
        ],
    )(spectral.reshape(2 * degrees, channels), legendre, pattern, assignment)


def grid_kernel(
    lats, received, synthesis, analysis, weight, returned, wide, ahead, back_rows, products
):
    blocks, rows, lanes = received.shape
    width = blocks * lanes
    slots = rows // (2 * lats)
    wide[...] = received[...].astype(jnp.float32)
    pair = 2 * lanes
    source = lax.broadcasted_iota(jnp.int32, (pair, pair), 0)
    target = lax.broadcasted_iota(jnp.int32, (pair, pair), 1)
    advance = (source == target // F * F + (target + 1) % F).astype(jnp.bfloat16)
    for i in range(0, blocks, 2):
        both = jnp.concatenate([received[i], received[i + 1]], axis=1)
        moved = jnp.dot(both, advance, preferred_element_type=jnp.float32)
        ahead[i] = moved[:, :lanes]
        ahead[i + 1] = moved[:, lanes:]

    def span(lat, part):
        return pl.ds(2 * lat + part, slots, stride=2 * lats)

    def gather(rows_of, lat):
        parts = [
            jnp.concatenate([rows_of[i, span(lat, part), :] for i in range(blocks)], axis=1)
            for part in range(2)
        ]
        return jnp.concatenate(parts, axis=0).astype(jnp.bfloat16)

    for lat in range(lats):
        field, partner = (
            jnp.dot(synthesis[...], gather(rows_of, lat), preferred_element_type=jnp.float32)
            for rows_of in (wide, ahead)
        )
        products[lat] = (field * partner).astype(jnp.bfloat16)
    for lat in range(lats):
        back = jnp.dot(analysis[...], products[lat], preferred_element_type=jnp.float32)
        back = back * weight[lat : lat + 1, :]
        for part in range(2):
            for i in range(blocks):
                back_rows[i, span(lat, part), :] = back[
                    part * slots : (part + 1) * slots, i * lanes : (i + 1) * lanes
                ]
    for i in range(blocks):
        returned[:, i * lanes : (i + 1) * lanes] = back_rows[i].astype(jnp.bfloat16)


def level_matrix(small, width):
    levels = small.shape[0]
    channel = lax.broadcasted_iota(jnp.int32, (width, levels), 0) // F
    level = lax.broadcasted_iota(jnp.int32, (width, levels), 1)
    spread = (channel == level).astype(jnp.bfloat16)
    contract = (((1,), (1,)), ((), ()))
    tall = lax.dot_general(spread, small, contract, preferred_element_type=jnp.float32)
    tall = tall.astype(jnp.bfloat16)
    full = lax.dot_general(tall, spread, contract, preferred_element_type=jnp.float32)
    source = lax.broadcasted_iota(jnp.int32, (width, width), 0) % F
    target = lax.broadcasted_iota(jnp.int32, (width, width), 1) % F
    return jnp.where(source == target, full, 0.0).astype(jnp.bfloat16)


def own_kernel(own, own_small, other_small, total, other_matrix):
    width = own.shape[1]
    total[...] = jnp.dot(
        own[...], level_matrix(own_small[...], width), preferred_element_type=jnp.float32
    )
    other_matrix[...] = level_matrix(other_small[...], width)


def couple_kernel(begun, other, other_matrix, sent):
    total = begun[...] + jnp.dot(other[...], other_matrix[...], preferred_element_type=jnp.float32)
    blocks, rows, lanes = sent.shape
    for i in range(blocks):
        sent[i] = total[:, i * lanes : (i + 1) * lanes].astype(jnp.bfloat16)


def backward_kernel(weighted, pruned_t, result, paired, coeffs, wide, merged, out_sem):
    degrees, lat_count = pruned_t.shape
    lanes = weighted.shape[1]
    paired[...] = weighted[...].astype(jnp.float32)
    for part in range(2):
        coeffs[:, part * lanes : (part + 1) * lanes] = paired[
            pl.ds(part, lat_count, stride=2), :
        ].astype(jnp.bfloat16)
    depth = degrees // 2
    founds = [
        jnp.dot(
            pruned_t[depth * j : depth * (j + 1), :],
            coeffs[...],
            preferred_element_type=jnp.float32,
        )
        for j in range(2)
    ]
    copies = []
    for j, found in enumerate(founds):
        for part in range(2):
            wide[pl.ds(2 * depth * j + part, depth, stride=2), :] = found[
                :, part * lanes : (part + 1) * lanes
            ]
        span = pl.ds(2 * depth * j, 2 * depth)
        merged[span, :] = wide[span, :].astype(jnp.bfloat16)
        copy = pltpu.make_async_copy(merged.at[span], result.at[span], out_sem.at[j])
        copy.start()
        copies.append(copy)
    for copy in copies:
        copy.wait()


def backward(weighted, pruned_t):
    degrees, lat_count = pruned_t.shape
    channels = weighted.shape[1]
    return pl.pallas_call(
        backward_kernel,
        out_shape=jax.ShapeDtypeStruct((2 * degrees, channels), jnp.bfloat16),
        in_specs=[pl.BlockSpec(memory_space=pltpu.VMEM)] * 2,
        out_specs=pl.BlockSpec(memory_space=pltpu.HBM),
        scratch_shapes=[
            pltpu.VMEM((2 * lat_count, channels), jnp.float32),
            pltpu.VMEM((lat_count, 2 * channels), jnp.bfloat16),
            pltpu.VMEM((2 * degrees, channels), jnp.float32),
            pltpu.VMEM((2 * degrees, channels), jnp.bfloat16),
            pltpu.SemaphoreType.DMA((2,)),
        ],
        compiler_params=pltpu.CompilerParams(vmem_limit_bytes=16 << 20),
    )(weighted, pruned_t)


def call(kernel, out_shape, flops, limit, *operands, scratch=()):
    arrays = (*operands, *jax.tree.leaves(out_shape))
    moved = sum(x.size * x.dtype.itemsize for x in arrays)
    return pl.pallas_call(
        kernel,
        out_shape=out_shape,
        in_specs=[pl.BlockSpec(memory_space=pltpu.VMEM)] * len(operands),
        out_specs=jax.tree.map(lambda _: pl.BlockSpec(memory_space=pltpu.VMEM), out_shape),
        scratch_shapes=scratch,
        compiler_params=pltpu.CompilerParams(vmem_limit_bytes=limit << 20),
        cost_estimate=pl.CostEstimate(flops=flops, bytes_accessed=moved, transcendentals=0),
    )(*operands)


def local(spectral, legendre, pattern, assignment, quad_weight, coupling):
    degrees = spectral.shape[1]
    channels = spectral.shape[3]
    lat_count = legendre.shape[1]
    wave_total = assignment.shape[0]
    y_count = SIZES["y"]
    peers = y_count * wave_total
    lats = lat_count // peers
    rows = wave_total * lats * 2
    own_levels = channels // F
    slot = lax.axis_index("z") * SIZES["x"] + lax.axis_index("x")
    core = lax.axis_index("core")

    own_wave = lax.dynamic_index_in_dim(assignment, slot, 0, keepdims=False)
    own_mask = lax.dynamic_index_in_dim(pattern, own_wave, 0, keepdims=False).astype(jnp.bfloat16)
    lat_tiles, deg_tiles = own_mask.shape
    wide_mask = jnp.broadcast_to(
        own_mask[:, None, :, None], (lat_tiles, TILE, deg_tiles, TILE)
    ).reshape(lat_count, degrees)
    pruned = legendre[0] * wide_mask

    at_lats = forward(spectral[0], legendre[0], pattern, assignment)
    at_lats = at_lats.reshape(peers, lats, 2, channels)
    received = exchange(at_lats)
    received = received.reshape(y_count, rows, channels)

    arrival = assignment.reshape(SIZES["z"], SIZES["x"])
    arrival = jnp.roll(arrival, (-middle("z"), -middle("x")), (0, 1)).T.reshape(wave_total)
    lon_count = 3 * wave_total
    synthesis, analysis = wave_tables(arrival, lon_count)
    cores = SIZES["core"]
    split = coupling.reshape(y_count, cores, own_levels, y_count, cores, own_levels)
    split = jnp.roll(split, (-middle("y"), -middle("y")), (0, 3))
    mine = lax.dynamic_index_in_dim(split, core, 1, keepdims=False)
    wide = y_count * channels

    def matrix(source):
        small = lax.dynamic_index_in_dim(mine, source, 3, keepdims=False)
        return small.reshape(wide // F, wide // F)

    group = own_position()
    weight = lax.dynamic_slice_in_dim(quad_weight, group * lats, lats)
    weight = jnp.broadcast_to(weight[:, None], (lats, wide))
    own_small, other_small = matrix(core), matrix(1 - core)
    received, synthesis, analysis, own_small, other_small, weight, pruned_t = (
        lax.optimization_barrier(
            (received, synthesis, analysis, own_small, other_small, weight, pruned.T)
        )
    )

    wide = y_count * channels
    flops = 4 * lon_count * rows * wide
    returned = call(
        functools.partial(grid_kernel, lats),
        jax.ShapeDtypeStruct((rows, wide), jnp.bfloat16),
        flops,
        16,
        received,
        synthesis,
        analysis,
        weight,
        scratch=[pltpu.VMEM((y_count, rows, channels), jnp.float32)] * 3
        + [pltpu.VMEM((lats, lon_count, wide), jnp.bfloat16)],
    )
    swapped = lax.ppermute(returned, "core", [(0, 1), (1, 0)])

    begun, other_matrix = call(
        own_kernel,
        (
            jax.ShapeDtypeStruct((rows, wide), jnp.float32),
            jax.ShapeDtypeStruct((wide, wide), jnp.bfloat16),
        ),
        2 * rows * wide * wide,
        16,
        returned,
        own_small,
        other_small,
    )
    sent = call(
        couple_kernel,
        jax.ShapeDtypeStruct((y_count, rows, channels), jnp.bfloat16),
        2 * rows * wide * wide,
        16,
        begun,
        swapped,
        other_matrix,
    )
    sent = sent.reshape(peers, lats, 2, channels)
    weighted = exchange(sent)
    tendency = backward(weighted.reshape(2 * lat_count, channels), pruned_t)
    return tendency.reshape(1, degrees, 2, channels)


def solution(mesh):
    grid = Mesh(mesh.devices.reshape(tuple(SIZES.values())), tuple(SIZES))
    wave, lev = ("z", "x"), ("y", "core")
    placed = (P(wave, None, None, lev), P(wave, None, None), P(), P(), P(), P())
    return jax.shard_map(
        local,
        mesh=grid,
        in_specs=placed,
        out_specs=P(wave, None, None, lev),
        check_vma=False,
    )
```
